256 devices in a mesh: seq: 32 (over x_lo, z, core), chan: 8 (over x_hi, y).
Axes of the slice: x: 4 (x_hi: 2, x_lo: 2; x = x_hi * 2 + x_lo), y: 4, z: 8, core: 2. Of those that a mesh axis runs over, the one named last changes fastest.
Arguments:
- inputs: bfloat16 [262144, 1024], P('seq', 'chan'), may hold values from -6 to 6
- out_grad: bfloat16 [262144, 1024], P('seq', 'chan'), may hold values from -6 to 6
- kernel: bfloat16 [512, 512, 1024], P('seq', None, 'chan'), may hold values from -4 to 4
- gate_weight: bfloat16 [1024, 1024], P(None, 'chan'), may hold values from -0.1875 to 0.1875
- right_factor: bfloat16 [512, 512], replicated, may hold values from -0.25 to 0.25
- left_factor: bfloat16 [512, 512], replicated, may hold values from -0.25 to 0.25
Outputs:
- input_grad: bfloat16 [262144, 1024], P('seq', 'chan')
- kernel_grad: bfloat16 [512, 512, 1024], P('seq', None, 'chan')
- right_grad: float32 [262144], P(('seq', 'chan'))
- left_grad: float32 [262144], P(('seq', 'chan'))
- gate_weight_grad: float32 [1024, 1024], P(('seq', 'chan'))
The draws below stay inside these ranges and needn't reach their ends.
All inputs are finite; a program needn't handle non-finite values.
Results may differ from the reference program's by a relative error of at most 0.015.
Values may be sent and summed in bfloat16 or wider, within the bound.
No kernel may reach another device: no remote copies, remote signals or barrier semaphores. Data moves between devices by JAX's collectives and lax.ppermute only.
A program may use at most 128 MiB of HBM per device.

```python
import jax
import jax.numpy as jnp
from jax import lax

BLOCK = 512
D = 1024
TOKENS = 262144


def levels(key, dims, split, low, high):
    factor_of = 1.0
    for position, shards_of in split:
        draws = jax.random.uniform(jax.random.fold_in(jax.random.fold_in(key, 6), position), (shards_of,), jnp.float32, low / len(split), high / len(split))
        factor_of = factor_of * jnp.repeat(jnp.exp(draws), dims[position] // shards_of).reshape((-1,) + (1,) * (len(dims) - 1 - position))
    return factor_of


def scatter_about(own_key, dims, width, reach, pieces=(), kind=jnp.bfloat16):
    entries = jax.random.normal(own_key, dims, jnp.float32) * width
    if len(pieces) > 0:
        entries = levels(own_key, dims, pieces, -0.22, 0.18) * entries
    return jnp.clip(entries, min=-reach, max=reach).astype(kind)


def setup_inputs(seed: int = 0) -> dict:
    keys = jax.random.split(jax.random.key(seed), 7)
    return {
        "inputs": scatter_about(keys[0], (TOKENS, D), 1.0, 6.0, ((0, 32), (1, 8))),
        "out_grad": scatter_about(keys[1], (TOKENS, D), 1.0, 6.0, ((0, 32), (1, 8))),
        "kernel": scatter_about(keys[2], (BLOCK, BLOCK, D), 1.0, 4.0, ((0, 32), (2, 8))),
        "gate_weight": scatter_about(keys[3], (D, D), D ** -0.5, 0.1875, ((1, 8),)),
        "right_factor": scatter_about(keys[4], (BLOCK, BLOCK), BLOCK ** -0.5, 0.25),
        "left_factor": scatter_about(keys[5], (BLOCK, BLOCK), BLOCK ** -0.5, 0.25),
    }


def reference(inputs, out_grad, kernel, gate_weight, right_factor, left_factor):
    pre = jnp.dot(inputs, gate_weight, preferred_element_type=jnp.float32)
    gate = jax.nn.sigmoid(pre).astype(jnp.bfloat16)
    blocks_in = inputs.reshape(BLOCK, BLOCK, D)
    cotangent = out_grad.reshape(BLOCK, BLOCK, D)
    gate_cube = gate.reshape(BLOCK, BLOCK, D)
    right_wide = right_factor.astype(jnp.float32)
    left_wide = left_factor.astype(jnp.float32)
    group = min(128, D)
    groups = D // group

    def one_group(carry, index):
        start = (index * group).astype(jnp.int32)
        xs_part = lax.dynamic_slice_in_dim(blocks_in, start, group, 2).astype(jnp.float32)
        ker_part = lax.dynamic_slice_in_dim(kernel, start, group, 2).astype(jnp.float32)
        gate_part = lax.dynamic_slice_in_dim(gate_cube, start, group, 2).astype(jnp.float32)
        cot_part = lax.dynamic_slice_in_dim(cotangent, start, group, 2).astype(jnp.float32)
        first = jnp.einsum('abc,jb->ajc', xs_part, right_wide).astype(jnp.bfloat16)
        scaled = (first.astype(jnp.float32) * ker_part).astype(jnp.bfloat16)
        mixed = jnp.einsum('ia,ajc->jic', left_wide, scaled.astype(jnp.float32)).astype(jnp.bfloat16)
        grad_mixed = (cot_part * gate_part).astype(jnp.bfloat16)
        grad_pre = (cot_part * mixed.astype(jnp.float32) * gate_part * (1.0 - gate_part)).astype(jnp.bfloat16)
        grad_mid = jnp.einsum('ia,jic->ajc', left_wide, grad_mixed.astype(jnp.float32)).astype(jnp.bfloat16)
        left_part = jnp.einsum('jic,ajc->ia', grad_mixed.astype(jnp.float32), scaled.astype(jnp.float32))
        grad_first = (grad_mid.astype(jnp.float32) * ker_part).astype(jnp.bfloat16)
        ker_grad = (grad_mid.astype(jnp.float32) * first.astype(jnp.float32)).astype(jnp.bfloat16)
        right_part = jnp.einsum('ajc,abc->jb', grad_first.astype(jnp.float32), xs_part)
        back = jnp.einsum('ajc,jb->abc', grad_first.astype(jnp.float32), right_wide)
        return ((carry[0] + right_part, carry[1] + left_part), (grad_pre, ker_grad, back))
    start_sums = (jnp.zeros((BLOCK, BLOCK), jnp.float32), jnp.zeros((BLOCK, BLOCK), jnp.float32))
    sums, stacked = lax.scan(one_group, start_sums, jnp.arange(groups, dtype=jnp.int32))
    right_raw, left_raw = sums
    grad_pre = jnp.moveaxis(stacked[0], 0, 2).reshape(TOKENS, D)
    kernel_grad = jnp.moveaxis(stacked[1], 0, 2).reshape(BLOCK, BLOCK, D)
    back = jnp.moveaxis(stacked[2], 0, 2).reshape(TOKENS, D)
    gate_input_grad = jnp.dot(grad_pre, gate_weight.T, preferred_element_type=jnp.float32).astype(jnp.bfloat16)
    weight_raw = jnp.dot(inputs.T, grad_pre, preferred_element_type=jnp.float32)
    input_grad = (back + gate_input_grad.astype(jnp.float32)).astype(jnp.bfloat16)
    factor_scale = 1.0 / jnp.sqrt(jnp.float32(BLOCK * D))
    token_scale = 1.0 / jnp.sqrt(jnp.float32(TOKENS))
    return (input_grad, kernel_grad, (right_raw * factor_scale).reshape(BLOCK * BLOCK), (left_raw * factor_scale).reshape(BLOCK * BLOCK), weight_raw * token_scale)
```

```python
import functools

import jax
import jax.numpy as jnp
from jax import lax
from jax.experimental import pallas as pl
from jax.experimental.pallas import tpu as pltpu
from jax.sharding import PartitionSpec as P

F32 = jnp.float32
BF16 = jnp.bfloat16
NT = (((1,), (1,)), ((), ()))


def call(body, name, grid, in_specs, out_specs, out_shape, scratch, flops, nbytes):
    return pl.pallas_call(
        body,
        name=name,
        grid_spec=pltpu.PrefetchScalarGridSpec(
            num_scalar_prefetch=1,
            grid=grid,
            in_specs=in_specs,
            out_specs=out_specs,
            scratch_shapes=scratch,
        ),
        out_shape=out_shape,
        cost_estimate=pl.CostEstimate(flops=flops, bytes_accessed=nbytes, transcendentals=0),
        compiler_params=pltpu.CompilerParams(vmem_limit_bytes=48 * 2**20),
    )


def lanes(parts):
    return jnp.concatenate(parts, axis=1)


def first_body(me, x_ref, k_ref, r_ref, u_ref, v_ref, scr, *, step):
    g = pl.program_id(0)
    heads, block = scr.shape[0] // r_ref.shape[0], r_ref.shape[0]
    rhs = lanes([x_ref[t] for t in range(step)])
    prod = jnp.dot(r_ref[...], rhs, preferred_element_type=F32).astype(BF16)
    for t in range(step):
        u = prod[:, t * 128 : (t + 1) * 128]
        u_ref[t] = u
        v = (u.astype(F32) * k_ref[t].astype(F32)).astype(BF16)
        scr[pl.ds(g * step + t, block, stride=heads), :] = v.astype(F32)

    @pl.when(g == pl.num_programs(0) - 1)
    def _():
        def put(s, carry):
            rows = scr[pl.ds(pl.multiple_of(s * heads * heads, 256), heads * heads), :]
            v_ref[s] = rows.reshape(heads, heads, 128).astype(BF16)
            return carry

        lax.fori_loop(0, v_ref.shape[0], put, 0)


def mix_body(me, p_ref, og_ref, l_ref, *outs):
    t = pl.program_id(0)
    block = l_ref.shape[0]
    rhs = lanes([p_ref[:, u].reshape(block, 128) for u in range(2)])
    mixed = jnp.dot(l_ref[...], rhs, preferred_element_type=F32).astype(BF16).astype(F32)
    both = jnp.concatenate(
        [(og_ref[u].astype(F32) * mixed[:, u * 128 : (u + 1) * 128]).astype(BF16) for u in range(2)],
        axis=0,
    )
    for q in range(len(outs)):

        @pl.when(t == q)
        def _(q=q):
            outs[q][...] = both


def gate_body(me, *refs, n):
    xs, ws, gs, wcat, scr = refs[:n], refs[n : 2 * n], refs[2 * n : 3 * n], refs[3 * n], refs[3 * n + 1]

    @pl.when(pl.program_id(0) == 0)
    def _():
        for r in range(n):
            rows = pl.ds(pl.multiple_of((me[0] ^ r) * 128, 128), 128)
            for q in range(n):
                scr[r * 128 : (r + 1) * 128, q * 128 : (q + 1) * 128] = ws[q][rows, :]
        wcat[...] = scr[...]

    rows_in = lanes([x[...] for x in xs])
    pre = jnp.dot(rows_in, scr[...], preferred_element_type=F32)
    gate = jax.nn.sigmoid(pre).astype(BF16)
    for q in range(n):
        gs[q][...] = gate[:, q * 128 : (q + 1) * 128]


def turn_body(me, *refs, n, own):
    xs, out = refs[:n], refs[n]
    g = pl.program_id(0)
    rows, width = out.shape[0], n * 128
    rho = lax.broadcasted_iota(jnp.int32, (rows, width), 0) + g * rows
    col = lax.broadcasted_iota(jnp.int32, (rows, width), 1)
    per = width // n
    inner = lax.rem(rho, per)
    want = (inner // own) * (own * n) + (me[0] ^ (rho // per)) * own + lax.rem(inner, own)
    have = (me[0] ^ (col // 128)) * 128 + lax.rem(col, 128)
    pick = jnp.where(want == have, 1.0, 0.0).astype(BF16)
    rows_in = lanes([x[...] for x in xs])
    out[...] = lax.dot_general(pick, rows_in, NT, preferred_element_type=F32).astype(BF16)


def back_gate_body(me, *refs, n):
    os, gs, wcat = refs[:n], refs[n : 2 * n], refs[2 * n]
    hs, gp_ref = refs[2 * n + 1 : 3 * n + 1], refs[3 * n + 1]
    parts = []
    for q in range(n):
        g = gs[q][...].astype(F32)
        parts.append((os[q][...].astype(F32) * g * (1.0 - g)).astype(BF16))
    gp = lanes(parts)
    gp_ref[...] = gp
    h = lax.dot_general(gp, wcat[...], NT, preferred_element_type=F32).astype(BF16)
    for r in range(n):
        hs[r][...] = h[:, r * 128 : (r + 1) * 128]


def weight_body(me, xt_ref, gp_ref, *outs):
    n = len(outs)
    g = pl.program_id(0)
    w = jnp.dot(xt_ref[...], gp_ref[...], preferred_element_type=F32).astype(BF16)
    per = xt_ref.shape[0] // 2
    for r in range(n):

        @pl.when(g == r // 2)
        def _(r=r):
            for q in range(n):
                cols = pl.ds(pl.multiple_of((me[0] ^ q) * 128, 128), 128)
                outs[r][:, cols] = w[(r % 2) * per : (r % 2 + 1) * per, q * 128 : (q + 1) * 128]


def cot_body(me, *refs, n):
    gs, og_ref, p_ref, lt_ref = refs[:n], refs[n], refs[n + 1], refs[n + 2]
    gv_ref, left_ref, gsc, acc = refs[n + 3 :]
    t = pl.program_id(0)
    block = lt_ref.shape[0]
    for q in range(n):

        @pl.when(t == q)
        def _(q=q):
            gsc[...] = gs[q][...]

    gm = lanes(
        [
            (og_ref[u].astype(F32) * gsc[u * block : (u + 1) * block, :].astype(F32)).astype(BF16)
            for u in range(2)
        ]
    )
    gv = jnp.dot(lt_ref[...], gm, preferred_element_type=F32).astype(BF16)
    for u in range(2):
        gv_ref[:, u] = gv[:, u * 128 : (u + 1) * 128].reshape(gv_ref.shape[0], gv_ref.shape[2], 128)
    piece = lanes([p_ref[:, u].reshape(block, 128) for u in range(2)])
    add = lax.dot_general(gm, piece, NT, preferred_element_type=F32)

    @pl.when(t == 0)
    def _():
        acc[...] = add

    @pl.when(t > 0)
    def _():
        acc[...] += add

    @pl.when(t == pl.num_programs(0) - 1)
    def _():
        left_ref[...] = acc[...].astype(BF16)


def kernel_grad_body(me, d_ref, u_ref, k_ref, x_ref, kg_ref, gu_ref, right_ref, scr, acc, *, heads):
    t = pl.program_id(0)
    block = u_ref.shape[1]

    @pl.when(t == 0)
    def _():
        def get(s, carry):
            rows = d_ref[s].astype(F32).reshape(heads * heads, 128)
            scr[pl.ds(pl.multiple_of(s * heads * heads, 256), heads * heads), :] = rows
            return carry

        lax.fori_loop(0, d_ref.shape[0], get, 0)

    gus = []
    for u in range(2):
        gv = scr[pl.ds(t * 2 + u, block, stride=heads), :]
        kg_ref[u] = (gv * u_ref[u].astype(F32)).astype(BF16)
        gu = (gv * k_ref[u].astype(F32)).astype(BF16)
        gu_ref[u] = gu
        gus.append(gu)
    add = lax.dot_general(
        lanes(gus), lanes([x_ref[u] for u in range(2)]), NT, preferred_element_type=F32
    )

    @pl.when(t == 0)
    def _():
        acc[...] = add

    @pl.when(t > 0)
    def _():
        acc[...] += add

    @pl.when(t == pl.num_programs(0) - 1)
    def _():
        right_ref[...] = acc[...].astype(BF16)


def input_grad_body(me, *refs, n):
    hs, gu_ref, rt_ref, out, hsc = refs[:n], refs[n], refs[n + 1], refs[n + 2], refs[n + 3]
    t = pl.program_id(0)
    block = rt_ref.shape[0]
    for q in range(n):

        @pl.when(t == q)
        def _(q=q):
            hsc[...] = hs[q][...]

    rhs = lanes([gu_ref[u] for u in range(2)])
    back = jnp.dot(rt_ref[...], rhs, preferred_element_type=F32)
    for u in range(2):
        rows = slice(u * block, (u + 1) * block)
        out[rows, :] = (back[:, u * 128 : (u + 1) * 128] + hsc[rows, :].astype(F32)).astype(BF16)


def local(inputs, out_grad, kernel, gate_weight, right_factor, left_factor):
    block = right_factor.shape[0]
    rows, width = inputs.shape
    model_width = gate_weight.shape[0]
    heads = rows // block
    seqs = block // heads
    n = model_width // width
    part = rows // n
    me = lax.axis_index("chan")
    pre = me.astype(jnp.int32).reshape(1)
    S = jax.ShapeDtypeStruct

    def swap(r, x):
        return x if r == 0 else lax.ppermute(x, "chan", [(i, i ^ r) for i in range(n)])

    def swaps(parts):
        return [swap(r, parts[r]) for r in range(n)]

    def whole(*shape):
        return pl.BlockSpec(shape, lambda t, me: (0,) * len(shape))

    mm = 2 * rows * block * width
    gg = 2 * part * model_width * model_width
    cube = rows * width * 2

    own = inputs.reshape(n, part, width)
    xs = swaps([lax.dynamic_index_in_dim(own, me ^ r, 0, keepdims=False) for r in range(n)])
    ws = swaps([gate_weight] * n)

    x_cube = inputs.reshape(heads, block, width)
    og_cube = out_grad.reshape(heads, block, width)
    step = 4
    first, scaled = call(
        functools.partial(first_body, step=step), "first", (heads // step,),
        [
            pl.BlockSpec((step, block, width), lambda g, me: (g, 0, 0)),
            pl.BlockSpec((step, block, width), lambda g, me: (g, 0, 0)),
            whole(block, block),
        ],
        [
            pl.BlockSpec((step, block, width), lambda g, me: (g, 0, 0)),
            whole(seqs, heads, heads, width),
        ],
        [S((heads, block, width), BF16), S((seqs, heads, heads, width), BF16)],
        [pltpu.VMEM((block * heads, width), F32)],
        mm, 4 * cube,
    )(pre, x_cube, kernel, right_factor)
    piece = lax.all_to_all(scaled, "seq", split_axis=0, concat_axis=0, tiled=True)

    chunk = part // 4 if part % 64 == 0 else part
    tok = pl.BlockSpec((chunk, width), lambda t, me: (t, 0))
    gate_out = call(
        functools.partial(gate_body, n=n), "gate", (part // chunk,),
        [tok] * n + [whole(model_width, width)] * n,
        [tok] * n + [whole(model_width, model_width)],
        [S((part, width), BF16)] * n + [S((model_width, model_width), BF16)],
        [pltpu.VMEM((model_width, model_width), BF16)],
        gg, 4 * cube,
    )(pre, *xs, *ws)
    gates_tok, wcat = gate_out[:n], gate_out[n]
    gates = swaps(gates_tok)

    pair_in = pl.BlockSpec((seqs, 2, heads, width), lambda t, me: (0, me[0] ^ t, 0, 0))
    pair_cube = pl.BlockSpec((2, block, width), lambda t, me: (me[0] ^ t, 0, 0))
    om = call(
        mix_body, "mix", (n,),
        [pair_in, pair_cube, whole(block, block)],
        [whole(part, width)] * n,
        [S((part, width), BF16)] * n,
        [],
        mm, 3 * cube,
    )(pre, piece, og_cube, left_factor)
    oms = swaps(om)

    turned = call(
        functools.partial(turn_body, n=n, own=model_width // (n * seqs)), "turn", (4,),
        [whole(part, width)] * n,
        pl.BlockSpec((model_width // 4, part), lambda t, me: (t, 0)),
        S((model_width, part), BF16),
        [],
        gg, 2 * cube,
    )(pre, *xs)

    grad_mid, left_part = call(
        functools.partial(cot_body, n=n), "cot", (n,),
        [whole(part, width)] * n + [pair_cube, pair_in, whole(block, block)],
        [pair_in, whole(block, block)],
        [S((seqs, heads, heads, width), BF16), S((block, block), BF16)],
        [pltpu.VMEM((part, width), BF16), pltpu.VMEM((block, block), F32)],
        2 * mm, 4 * cube,
    )(pre, *gates, og_cube, piece, left_factor.T)
    grad_back = lax.all_to_all(grad_mid, "seq", split_axis=0, concat_axis=0, tiled=True)

    back_out = call(
        functools.partial(back_gate_body, n=n), "back_gate", (part // chunk,),
        [tok] * n + [tok] * n + [whole(model_width, model_width)],
        [tok] * n + [pl.BlockSpec((chunk, model_width), lambda t, me: (t, 0))],
        [S((part, width), BF16)] * n + [S((part, model_width), BF16)],
        [],
        gg, 5 * cube,
    )(pre, *oms, *gates_tok, wcat)
    hs = swaps(back_out[:n])
    grad_pre = back_out[n]

    wparts = call(
        weight_body, "weight", (4,),
        [
            pl.BlockSpec((model_width // 4, part), lambda t, me: (t, 0)),
            whole(part, model_width),
        ],
        [whole(model_width // n, model_width)] * n,
        [S((model_width // n, model_width), BF16)] * n,
        [],
        gg, 3 * cube,
    )(pre, turned, grad_pre)
    wgot = swaps(wparts)
    wsum = functools.reduce(lambda a, b: a + b, [w.astype(F32) for w in wgot]).astype(BF16)

    kernel_grad, grad_first, right_part = call(
        functools.partial(kernel_grad_body, heads=heads), "kernel_grad", (heads // 2,),
        [whole(seqs, heads, heads, width)]
        + [pl.BlockSpec((2, block, width), lambda t, me: (t, 0, 0))] * 3,
        [pl.BlockSpec((2, block, width), lambda t, me: (t, 0, 0))] * 2 + [whole(block, block)],
        [S((heads, block, width), BF16)] * 2 + [S((block, block), BF16)],
        [pltpu.VMEM((block * heads, width), F32), pltpu.VMEM((block, block), F32)],
        mm, 6 * cube,
    )(pre, grad_back, first, kernel, x_cube)

    input_grad = call(
        functools.partial(input_grad_body, n=n), "input_grad", (n,),
        [whole(part, width)] * n + [pair_cube, whole(block, block)],
        pl.BlockSpec((part, width), lambda t, me: (me[0] ^ t, 0)),
        S((rows, width), BF16),
        [pltpu.VMEM((part, width), BF16)],
        mm, 3 * cube,
    )(pre, *hs, grad_first, right_factor.T)

    def over_seq(x):
        got = lax.all_to_all(x, "seq", split_axis=0, concat_axis=0, tiled=True)
        return jnp.sum(got.astype(F32), axis=0)

    left_rows = over_seq(left_part.reshape(seqs, heads, block))
    right_rows = over_seq(right_part.reshape(seqs, heads, block))
    weight_share = over_seq(wsum.reshape(seqs, model_width // n // seqs, model_width))
    both = jnp.stack([left_rows, right_rows], axis=1).astype(BF16)
    both = both.reshape(n, heads // n, 2, block)
    got = lax.all_to_all(both, "chan", split_axis=0, concat_axis=0, tiled=True)
    shares = jnp.sum(got.astype(F32), axis=0)
    left_share = shares[:, 0].reshape(-1)
    right_share = shares[:, 1].reshape(-1)
    factor_scale = 1.0 / jnp.sqrt(jnp.float32(block * model_width))
    token_scale = 1.0 / jnp.sqrt(jnp.float32(block * block))
    return (
        input_grad,
        kernel_grad,
        right_share * factor_scale,
        left_share * factor_scale,
        weight_share * token_scale,
    )


def solution(mesh):
    in_specs = (
        P("seq", "chan"),
        P("seq", "chan"),
        P("seq", None, "chan"),
        P(None, "chan"),
        P(),
        P(),
    )
    out_specs = (
        P("seq", "chan"),
        P("seq", None, "chan"),
        P(("seq", "chan")),
        P(("seq", "chan")),
        P(("seq", "chan"), None),
    )
    return jax.shard_map(local, mesh=mesh, in_specs=in_specs, out_specs=out_specs, check_vma=False)
```

```python
import functools

import jax
import jax.numpy as jnp
from jax import lax
from jax.experimental import pallas as pl
from jax.experimental.pallas import tpu as pltpu
from jax.sharding import PartitionSpec as P

F32 = jnp.float32
BF16 = jnp.bfloat16
NT = (((1,), (1,)), ((), ()))


def call(body, name, grid, in_specs, out_specs, out_shape, scratch, flops, nbytes):
    return pl.pallas_call(
        body,
        name=name,
        grid_spec=pltpu.PrefetchScalarGridSpec(
            num_scalar_prefetch=1,
            grid=grid,
            in_specs=in_specs,
            out_specs=out_specs,
            scratch_shapes=scratch,
        ),
        out_shape=out_shape,
        cost_estimate=pl.CostEstimate(flops=flops, bytes_accessed=nbytes, transcendentals=0),
        compiler_params=pltpu.CompilerParams(vmem_limit_bytes=48 * 2**20),
    )


def lanes(parts):
    return jnp.concatenate(parts, axis=1)


def first_body(me, x_ref, k_ref, r_ref, tie, u_ref, v_ref, scr, *, step):
    g = pl.program_id(0)
    heads, block = scr.shape[0] // r_ref.shape[0], r_ref.shape[0]
    rhs = lanes([x_ref[t] for t in range(step)])
    prod = jnp.dot(r_ref[...], rhs, preferred_element_type=F32).astype(BF16)
    for t in range(step):
        u = prod[:, t * 128 : (t + 1) * 128]
        u_ref[t] = u
        v = (u.astype(F32) * k_ref[t].astype(F32)).astype(BF16)
        scr[pl.ds(g * step + t, block, stride=heads), :] = v.astype(F32)

    @pl.when(g == pl.num_programs(0) - 1)
    def _():
        def put(s, carry):
            rows = scr[pl.ds(pl.multiple_of(s * heads * heads, 256), heads * heads), :]
            v_ref[s] = rows.reshape(heads, heads, 128).astype(BF16)
            return carry

        lax.fori_loop(0, v_ref.shape[0], put, 0)


def mix_body(me, p_ref, og_ref, l_ref, *outs):
    t = pl.program_id(0)
    block = l_ref.shape[0]
    rhs = lanes([p_ref[:, u].reshape(block, 128) for u in range(2)])
    mixed = jnp.dot(l_ref[...], rhs, preferred_element_type=F32).astype(BF16).astype(F32)
    both = jnp.concatenate(
        [(og_ref[u].astype(F32) * mixed[:, u * 128 : (u + 1) * 128]).astype(BF16) for u in range(2)],
        axis=0,
    )
    for q in range(len(outs)):

        @pl.when(t == q)
        def _(q=q):
            outs[q][...] = both


def gate_body(me, x_ref, w_ref, mine_ref, peer_ref, *refs, n):
    gs, wcat, scr = refs[:n], refs[n], refs[n + 1]

    @pl.when(pl.program_id(0) == 0)
    def _():
        half = w_ref.shape[0] // 2
        near = pl.ds(pl.multiple_of(me[1] * half, half), half)
        far = pl.ds(pl.multiple_of((1 - me[1]) * half, half), half)
        scr[:, :128] = w_ref[...]
        for q in range(1, n):
            scr[near, q * 128 : (q + 1) * 128] = mine_ref[q - 1]
            scr[far, q * 128 : (q + 1) * 128] = peer_ref[q - 1]
        wcat[...] = scr[...]

    rows_in = lanes([x_ref[r] for r in range(n)])
    pre = jnp.dot(rows_in, scr[...], preferred_element_type=F32)
    gate = jax.nn.sigmoid(pre).astype(BF16)
    for q in range(n):
        gs[q][...] = gate[:, q * 128 : (q + 1) * 128]


def turn_body(me, x_ref, out, *, n, seqs):
    g = pl.program_id(0)
    rows, width = out.shape[0], n * 128
    rho = lax.broadcasted_iota(jnp.int32, (rows, width), 0) + g * rows
    col = lax.broadcasted_iota(jnp.int32, (rows, width), 1)
    per = width // (2 * n)
    high = seqs // 2
    own = per // high
    core = me[1] ^ (rho // (width // 2))
    rest = lax.rem(rho, width // 2)
    inner = lax.rem(rest, per)
    seq = lax.rem(inner, high) * 2 + core
    want = (seq * n + (me[0] ^ (rest // per))) * own + inner // high
    pick = jnp.where(want == col, 1.0, 0.0).astype(BF16)
    rows_in = lanes([x_ref[r] for r in range(n)])
    out[...] = lax.dot_general(pick, rows_in, NT, preferred_element_type=F32).astype(BF16)


def back_gate_body(me, *refs, n):
    os, gs, wcat, left_ref = refs[:n], refs[n : 2 * n], refs[2 * n], refs[2 * n + 1]
    hs, gp_ref, hsc = refs[2 * n + 2 : 3 * n + 2], refs[3 * n + 2], refs[3 * n + 3]
    t = pl.program_id(0)
    chunk = gp_ref.shape[0]
    rows = pl.ds(pl.multiple_of(t * chunk, chunk), chunk)
    parts = []
    for q in range(n):
        g = gs[q][...].astype(F32)
        parts.append((os[q][...].astype(F32) * g * (1.0 - g)).astype(BF16))
    gp = lanes(parts)
    gp_ref[...] = gp
    hsc[...] = lax.dot_general(gp, wcat[...], NT, preferred_element_type=F32).astype(BF16)
    for r in range(n):
        hs[r][rows, :] = hsc[:, pl.ds(pl.multiple_of((me[0] ^ r) * 128, 128), 128)]

    @pl.when(t == 0)
    def _():
        base = hs[0].shape[0] - left_ref.shape[1]
        for r in range(n):
            hs[r][base:, :] = left_ref[r]


def weight_body(me, xt_ref, gp_ref, mine, peer, *, n):
    g = pl.program_id(0)
    w = jnp.dot(xt_ref[...], gp_ref[...], preferred_element_type=F32).astype(BF16)

    def put(out):
        for q in range(n):
            cols = pl.ds(pl.multiple_of((me[0] ^ q) * 128, 128), 128)
            out[:, cols] = w[:, q * 128 : (q + 1) * 128]

    @pl.when(g < 2)
    def _():
        put(mine)

    @pl.when(g >= 2)
    def _():
        put(peer)


def add_body(me, a_ref, b_ref, *outs):
    per = outs[0].shape[0]
    for r in range(len(outs)):
        rows = slice(r * per, (r + 1) * per)
        outs[r][...] = (a_ref[rows, :].astype(F32) + b_ref[rows, :].astype(F32)).astype(BF16)


def row_order(me, block, n, seqs):
    rho = lax.broadcasted_iota(jnp.int32, (block, block), 0)
    col = lax.broadcasted_iota(jnp.int32, (block, block), 1)
    per = block // n
    own = per // seqs
    inner = lax.rem(rho, per)
    want = (lax.rem(inner, seqs) * n + (me[0] ^ (rho // per))) * own + inner // seqs
    return jnp.where(want == col, 1.0, 0.0).astype(BF16)


def put_rows(me, acc, n, seqs, put):
    block = acc.shape[0]
    sums = jnp.dot(
        row_order(me, block, n, seqs), acc[...].astype(BF16), preferred_element_type=F32
    ).astype(BF16)
    per = block // n
    for r in range(n):
        for t in range(per // seqs):
            for m in range(block // 128):
                slot = t * (block // 128) + m
                low = r * per + t * seqs
                put(r, slot * seqs, sums[low : low + seqs, m * 128 : (m + 1) * 128])


def gate_pick(t, gs, gsc):
    for q in range(len(gs)):

        @pl.when(t == q)
        def _(q=q):
            gsc[...] = gs[q][...]


def grad_mixed_of(og_ref, gsc, block):
    return lanes(
        [
            (og_ref[u].astype(F32) * gsc[u * block : (u + 1) * block, :].astype(F32)).astype(BF16)
            for u in range(2)
        ]
    )


def cot_body(me, *refs, n):
    gs, og_ref, lt_ref, gv_ref, gm_ref, gsc = refs[:n], *refs[n:]
    block = lt_ref.shape[0]
    gate_pick(pl.program_id(0), gs, gsc)
    gm = grad_mixed_of(og_ref, gsc, block)
    gm_ref[...] = gm
    gv = jnp.dot(lt_ref[...], gm, preferred_element_type=F32).astype(BF16)
    for u in range(2):
        gv_ref[:, u] = gv[:, u * 128 : (u + 1) * 128].reshape(gv_ref.shape[0], gv_ref.shape[2], 128)


def accumulate(acc, t, add):
    @pl.when(t == 0)
    def _():
        acc[...] = add

    @pl.when(t > 0)
    def _():
        acc[...] += add


def left_body(me, gm_ref, p_ref, tie, out, acc, *, n, seqs):
    t = pl.program_id(0)
    block = acc.shape[0]
    pairs = gm_ref.shape[0]
    gm = lanes([gm_ref[v] for v in range(pairs)])
    piece = lanes([p_ref[:, u].reshape(block, 128) for u in range(2 * pairs)])
    accumulate(acc, t, lax.dot_general(gm, piece, NT, preferred_element_type=F32))

    @pl.when(t == pl.num_programs(0) - 1)
    def _():
        def put(r, row, value):
            out[r, row : row + seqs, :] = value

        put_rows(me, acc, n, seqs, put)


def kernel_grad_body(me, d_ref, u_ref, k_ref, x_ref, kg_ref, gu_ref, *refs, heads, n, seqs):
    outs, scr, acc = refs[:n], refs[n], refs[n + 1]
    t = pl.program_id(0)
    step, block = u_ref.shape[0], u_ref.shape[1]

    @pl.when(t == 0)
    def _():
        def get(s, carry):
            rows = d_ref[s].astype(F32).reshape(heads * heads, 128)
            scr[pl.ds(pl.multiple_of(s * heads * heads, 256), heads * heads), :] = rows
            return carry

        lax.fori_loop(0, d_ref.shape[0], get, 0)

    gus = []
    for u in range(step):
        gv = scr[pl.ds(t * step + u, block, stride=heads), :]
        kg_ref[u] = (gv * u_ref[u].astype(F32)).astype(BF16)
        gu = (gv * k_ref[u].astype(F32)).astype(BF16)
        gu_ref[u] = gu
        gus.append(gu)
    accumulate(
        acc,
        t,
        lax.dot_general(
            lanes(gus), lanes([x_ref[u] for u in range(step)]), NT, preferred_element_type=F32
        ),
    )

    @pl.when(t == pl.num_programs(0) - 1)
    def _():
        def put(r, row, value):
            outs[r][row : row + seqs, :] = value

        put_rows(me, acc, n, seqs, put)


def input_grad_body(me, *refs, n):
    hs, gu_ref, rt_ref, out, hsc = refs[:n], refs[n], refs[n + 1], refs[n + 2], refs[n + 3]
    block = rt_ref.shape[0]
    gate_pick(pl.program_id(0), hs, hsc)
    rhs = lanes([gu_ref[u] for u in range(2)])
    back = jnp.dot(rt_ref[...], rhs, preferred_element_type=F32)
    for u in range(2):
        rows = slice(u * block, (u + 1) * block)
        out[rows, :] = (back[:, u * 128 : (u + 1) * 128] + hsc[rows, :].astype(F32)).astype(BF16)


def total(parts):
    return functools.reduce(lambda a, b: a + b, [p.astype(F32) for p in parts])


def pack_body(me, *refs, n, seqs):
    lefts, rights, ws, out, scr = refs[:n], refs[n : 2 * n], refs[2 * n : 3 * n], refs[3 * n], refs[3 * n + 1]
    slots = out.shape[1]
    left, right, weight = [total([r[...] for r in group]) for group in (lefts, rights, ws)]
    count = left.shape[0] // seqs
    for slot in range(count):
        rows = slice(slot * seqs, (slot + 1) * seqs)
        scr[pl.ds(slot, seqs, stride=slots), :] = left[rows]
        scr[pl.ds(count + slot, seqs, stride=slots), :] = right[rows]
    high = seqs // 2
    blocks = weight.shape[1] // 128
    zero = jnp.zeros((high, 128), F32)
    for t in range(weight.shape[0] // high):
        for m in range(blocks):
            slot = 2 * count + t * blocks + m
            value = weight[t * high : (t + 1) * high, m * 128 : (m + 1) * 128]
            scr[pl.ds(slot + me[1] * slots, high, stride=2 * slots), :] = value
            scr[pl.ds(slot + (1 - me[1]) * slots, high, stride=2 * slots), :] = zero

    def emit(s, carry):
        out[s] = scr[pl.ds(pl.multiple_of(s * slots, 16), slots), :].astype(BF16)
        return carry

    lax.fori_loop(0, seqs, emit, 0)


def share_body(me, p_ref, left_ref, right_ref, weight_ref, *, factor, token):
    sums = lax.fori_loop(
        1, p_ref.shape[0], lambda s, acc: acc + p_ref[s].astype(F32), p_ref[0].astype(F32)
    )
    count = left_ref.shape[0]
    left_ref[...] = sums[:count] * factor
    right_ref[...] = sums[count : 2 * count] * factor
    weight_ref[...] = sums[2 * count :] * token


def local(inputs, out_grad, kernel, gate_weight, right_factor, left_factor):
    block = right_factor.shape[0]
    rows, width = inputs.shape
    model_width = gate_weight.shape[0]
    heads = rows // block
    seqs = block // heads
    n = model_width // width
    part = rows // n
    chan = lax.axis_index("chan")
    core = lax.axis_index("seq") % 2
    pre = jnp.stack([chan, core]).astype(jnp.int32)
    S = jax.ShapeDtypeStruct

    def swap(r, x):
        return x if r == 0 else lax.ppermute(x, "chan", [(i, i ^ r) for i in range(n)])

    def swaps(parts):
        return [swap(r, parts[r]) for r in range(n)]

    def across(x):
        return lax.ppermute(x, "seq", [(i, i ^ 1) for i in range(seqs)])

    def whole(*shape):
        return pl.BlockSpec(shape, lambda t, me: (0,) * len(shape))

    tie = pl.BlockSpec(memory_space=pl.ANY)
    mm = 2 * rows * block * width
    gg = 2 * part * model_width * model_width
    cube = rows * width * 2

    xs = lax.all_to_all(
        inputs.reshape(n, part, width), "chan", split_axis=0, concat_axis=0, tiled=True
    )
    half = lax.dynamic_slice_in_dim(gate_weight, core * (model_width // 2), model_width // 2, 0)
    near = jnp.stack([swap(r, half) for r in range(1, n)])
    far = across(near)

    x_cube = inputs.reshape(heads, block, width)
    og_cube = out_grad.reshape(heads, block, width)
    step = 4
    four = pl.BlockSpec((step, block, width), lambda g, me: (g, 0, 0))
    first, scaled = call(
        functools.partial(first_body, step=step), "first", (heads // step,),
        [four, four, whole(block, block), tie],
        [four, whole(seqs, heads, heads, width)],
        [S((heads, block, width), BF16), S((seqs, heads, heads, width), BF16)],
        [pltpu.VMEM((block * heads, width), F32)],
        mm, 4 * cube,
    )(pre, x_cube, kernel, right_factor, far)
    piece = lax.all_to_all(scaled, "seq", split_axis=0, concat_axis=0, tiled=True)

    chunk = part // 4
    tok = pl.BlockSpec((chunk, width), lambda t, me: (t, 0))
    gate_out = call(
        functools.partial(gate_body, n=n), "gate", (part // chunk,),
        [
            pl.BlockSpec((n, chunk, width), lambda t, me: (0, t, 0)),
            whole(model_width, width),
            whole(n - 1, model_width // 2, width),
            whole(n - 1, model_width // 2, width),
        ],
        [tok] * n + [whole(model_width, model_width)],
        [S((part, width), BF16)] * n + [S((model_width, model_width), BF16)],
        [pltpu.VMEM((model_width, model_width), BF16)],
        gg, 4 * cube,
    )(pre, xs, gate_weight, near, far)
    gates_tok, wcat = gate_out[:n], gate_out[n]
    gates = swaps(gates_tok)

    pair_in = pl.BlockSpec((seqs, 2, heads, width), lambda t, me: (0, me[0] ^ t, 0, 0))
    pair_cube = pl.BlockSpec((2, block, width), lambda t, me: (me[0] ^ t, 0, 0))
    grad_mid, grad_mixed = call(
        functools.partial(cot_body, n=n), "cot", (n,),
        [whole(part, width)] * n + [pair_cube, whole(block, block)],
        [pair_in, pl.BlockSpec((None, block, 2 * width), lambda t, me: (me[0] ^ t, 0, 0))],
        [S((seqs, heads, heads, width), BF16), S((n, block, 2 * width), BF16)],
        [pltpu.VMEM((part, width), BF16)],
        mm, 4 * cube,
    )(pre, *gates, og_cube, left_factor.T)
    grad_back = lax.all_to_all(grad_mid, "seq", split_axis=0, concat_axis=0, tiled=True)

    om = call(
        mix_body, "mix", (n,),
        [pair_in, pair_cube, whole(block, block)],
        [whole(part, width)] * n,
        [S((part, width), BF16)] * n,
        [],
        mm, 3 * cube,
    )(pre, piece, og_cube, left_factor)
    oms = swaps(om)

    count = block * block // (n * seqs * 128)
    lefts = call(
        functools.partial(left_body, n=n, seqs=seqs), "left", (n // 2,),
        [
            pl.BlockSpec((2, block, 2 * width), lambda t, me: (t, 0, 0)),
            pl.BlockSpec((seqs, 4, heads, width), lambda t, me: (0, t, 0, 0)),
            tie,
        ],
        whole(n, count * seqs, 128),
        S((n, count * seqs, 128), BF16),
        [pltpu.VMEM((block, block), F32)],
        mm, 2 * cube,
    )(pre, grad_mixed, piece, om[0])

    turned = call(
        functools.partial(turn_body, n=n, seqs=seqs), "turn", (4,),
        [whole(n, part, width)],
        pl.BlockSpec((model_width // 4, part), lambda t, me: (t, 0)),
        S((model_width, part), BF16),
        [],
        gg, 2 * cube,
    )(pre, xs)

    tall = part + count * seqs
    back_out = call(
        functools.partial(back_gate_body, n=n), "back_gate", (part // chunk,),
        [tok] * n + [tok] * n + [whole(model_width, model_width), whole(n, count * seqs, 128)],
        [whole(tall, width)] * n + [pl.BlockSpec((chunk, model_width), lambda t, me: (t, 0))],
        [S((tall, width), BF16)] * n + [S((part, model_width), BF16)],
        [pltpu.VMEM((chunk, model_width), BF16)],
        gg, 5 * cube,
    )(pre, *oms, *gates_tok, wcat, lefts)
    hs = swaps(back_out[:n])
    grad_pre = back_out[n]

    quarter = (model_width // 4, model_width)
    mine, other = call(
        functools.partial(weight_body, n=n), "weight", (4,),
        [
            pl.BlockSpec((model_width // 4, part), lambda t, me: (t, 0)),
            whole(part, model_width),
        ],
        [
            pl.BlockSpec(quarter, lambda t, me: (jnp.minimum(t, 1), 0)),
            pl.BlockSpec(quarter, lambda t, me: (jnp.maximum(t - 2, 0), 0)),
        ],
        [S((model_width // 2, model_width), BF16)] * 2,
        [],
        gg, 3 * cube,
    )(pre, turned, grad_pre)
    strip = (model_width // (2 * n), model_width)
    wparts = call(
        add_body, "add", (1,),
        [whole(model_width // 2, model_width)] * 2,
        [whole(*strip)] * n,
        [S(strip, BF16)] * n,
        [],
        cube, 2 * cube,
    )(pre, mine, across(other))
    wgot = swaps(wparts)

    kernel_out = call(
        functools.partial(kernel_grad_body, heads=heads, n=n, seqs=seqs), "kernel_grad", (heads // step,),
        [whole(seqs, heads, heads, width), four, four, four],
        [four, four] + [whole(count * seqs, 128)] * n,
        [S((heads, block, width), BF16)] * 2 + [S((count * seqs, 128), BF16)] * n,
        [pltpu.VMEM((block * heads, width), F32), pltpu.VMEM((block, block), F32)],
        mm, 6 * cube,
    )(pre, grad_back, first, kernel, x_cube)
    kernel_grad, grad_first = kernel_out[:2]
    rights = swaps(kernel_out[2:])

    slots = 2 * count + model_width * model_width // (n * seqs * 128)
    packed = call(
        functools.partial(pack_body, n=n, seqs=seqs), "pack", (1,),
        [pl.BlockSpec((count * seqs, 128), lambda t, me: (part // (count * seqs), 0))] * n
        + [whole(count * seqs, 128)] * n
        + [whole(*strip)] * n,
        whole(seqs, slots, 128),
        S((seqs, slots, 128), BF16),
        [pltpu.VMEM((seqs * slots, 128), F32)],
        cube, 2 * cube,
    )(pre, *hs, *rights, *wgot)
    got = lax.all_to_all(packed, "seq", split_axis=0, concat_axis=0, tiled=True)

    input_grad = call(
        functools.partial(input_grad_body, n=n), "input_grad", (n,),
        [whole(part, width)] * n + [pair_cube, whole(block, block)],
        pl.BlockSpec((part, width), lambda t, me: (me[0] ^ t, 0)),
        S((rows, width), BF16),
        [pltpu.VMEM((part, width), BF16)],
        mm, 3 * cube,
    )(pre, *hs, grad_first, right_factor.T)

    left_share, right_share, weight_share = call(
        functools.partial(
            share_body, factor=(block * model_width) ** -0.5, token=1.0 / block
        ), "share", (1,),
        [whole(seqs, slots, 128)],
        [whole(count, 128), whole(count, 128), whole(slots - 2 * count, 128)],
        [S((count, 128), F32), S((count, 128), F32), S((slots - 2 * count, 128), F32)],
        [],
        cube, cube,
    )(pre, got)
    return (
        input_grad,
        kernel_grad,
        right_share.reshape(-1),
        left_share.reshape(-1),
        weight_share.reshape(-1, model_width),
    )


def solution(mesh):
    in_specs = (
        P("seq", "chan"),
        P("seq", "chan"),
        P("seq", None, "chan"),
        P(None, "chan"),
        P(),
        P(),
    )
    out_specs = (
        P("seq", "chan"),
        P("seq", None, "chan"),
        P(("seq", "chan")),
        P(("seq", "chan")),
        P(("seq", "chan"), None),
    )
    return jax.shard_map(local, mesh=mesh, in_specs=in_specs, out_specs=out_specs, check_vma=False)
```

```python
import functools

import jax
import jax.numpy as jnp
from jax import lax
from jax.experimental import pallas as pl
from jax.experimental.pallas import tpu as pltpu
from jax.sharding import PartitionSpec as P


F32 = jnp.float32
BF16 = jnp.bfloat16
NT = (((1,), (1,)), ((), ()))


def call(body, grid, in_specs, out_specs, out_shape, scratch, flops, nbytes):
    return pl.pallas_call(
        body,
        grid_spec=pltpu.PrefetchScalarGridSpec(
            num_scalar_prefetch=1,
            grid=grid,
            in_specs=in_specs,
            out_specs=out_specs,
            scratch_shapes=scratch,
        ),
        out_shape=out_shape,
        cost_estimate=pl.CostEstimate(flops=flops, bytes_accessed=nbytes, transcendentals=0),
    )


def lanes(parts):
    return jnp.concatenate(parts, axis=1)


def first_body(me, x_ref, k_ref, r_ref, tie, u_ref, v_ref, scr, *, step):
    g = pl.program_id(0)
    heads, block = scr.shape[0] // r_ref.shape[0], r_ref.shape[0]
    rhs = lanes([x_ref[t] for t in range(step)])
    prod = jnp.dot(r_ref[...], rhs, preferred_element_type=F32).astype(BF16)
    for t in range(step):
        u = prod[:, t * 128 : (t + 1) * 128]
        u_ref[t] = u
        v = (u.astype(F32) * k_ref[t].astype(F32)).astype(BF16)
        scr[pl.ds(g * step + t, block, stride=heads), :] = v.astype(F32)

    @pl.when(g == pl.num_programs(0) - 1)
    def _():
        def put(s, carry):
            rows = scr[pl.ds(pl.multiple_of(s * heads * heads, 256), heads * heads), :]
            v_ref[s] = rows.reshape(heads, heads, 128).astype(BF16)
            return carry

        lax.fori_loop(0, v_ref.shape[0], put, 0)


def mix_body(me, p_ref, og_ref, l_ref, *outs):
    t = pl.program_id(0)
    block = l_ref.shape[0]
    rhs = lanes([p_ref[:, u].reshape(block, 128) for u in range(2)])
    mixed = jnp.dot(l_ref[...], rhs, preferred_element_type=F32).astype(BF16).astype(F32)
    both = jnp.concatenate(
        [(og_ref[u].astype(F32) * mixed[:, u * 128 : (u + 1) * 128]).astype(BF16) for u in range(2)],
        axis=0,
    )
    for q in range(len(outs)):

        @pl.when(t == q)
        def _(q=q):
            outs[q][...] = both


def gate_body(me, x_ref, w_ref, mine_ref, peer_ref, *refs, n):
    gs, wcat, scr = refs[:n], refs[n], refs[n + 1]

    @pl.when(pl.program_id(0) == 0)
    def _():
        half = w_ref.shape[0] // 2
        near = pl.ds(pl.multiple_of(me[1] * half, half), half)
        far = pl.ds(pl.multiple_of((1 - me[1]) * half, half), half)
        scr[:, :128] = w_ref[...]
        for q in range(1, n):
            scr[near, q * 128 : (q + 1) * 128] = mine_ref[q - 1]
            scr[far, q * 128 : (q + 1) * 128] = peer_ref[q - 1]
        wcat[...] = scr[...]

    rows_in = lanes([x_ref[r] for r in range(n)])
    pre = jnp.dot(rows_in, scr[...], preferred_element_type=F32)
    gate = jax.nn.sigmoid(pre).astype(BF16)
    for q in range(n):
        gs[q][...] = gate[:, q * 128 : (q + 1) * 128]


def turn_body(me, x_ref, out, *, n, seqs):
    g = pl.program_id(0)
    rows, width = out.shape[0], n * 128
    rho = lax.broadcasted_iota(jnp.int32, (rows, width), 0) + g * rows
    col = lax.broadcasted_iota(jnp.int32, (rows, width), 1)
    per = width // (2 * n)
    high = seqs // 2
    own = per // high
    core = me[1] ^ (rho // (width // 2))
    rest = lax.rem(rho, width // 2)
    inner = lax.rem(rest, per)
    seq = lax.rem(inner, high) * 2 + core
    want = (seq * n + (me[0] ^ (rest // per))) * own + inner // high
    pick = jnp.where(want == col, 1.0, 0.0).astype(BF16)
    rows_in = lanes([x_ref[r] for r in range(n)])
    out[...] = lax.dot_general(pick, rows_in, NT, preferred_element_type=F32).astype(BF16)


def back_gate_body(me, *refs, n):
    os, gs, wcat, tie, h_ref, gp_ref = refs[:n], refs[n : 2 * n], *refs[2 * n :]
    parts = []
    for q in range(n):
        g = gs[q][...].astype(F32)
        parts.append((os[q][...].astype(F32) * g * (1.0 - g)).astype(BF16))
    gp = lanes(parts)
    gp_ref[...] = gp
    h = lax.dot_general(gp, wcat[...], NT, preferred_element_type=F32).astype(BF16)
    for d in range(n):
        h_ref[d] = h[:, d * 128 : (d + 1) * 128]


def weight_body(me, xt_ref, gp_ref, mine, peer, *, n):
    g = pl.program_id(0)
    w = jnp.dot(xt_ref[...], gp_ref[...], preferred_element_type=F32).astype(BF16)

    def put(out):
        for q in range(n):
            cols = pl.ds(pl.multiple_of((me[0] ^ q) * 128, 128), 128)
            out[:, cols] = w[:, q * 128 : (q + 1) * 128]

    @pl.when(g < 2)
    def _():
        put(mine)

    @pl.when(g >= 2)
    def _():
        put(peer)


def add_body(me, a_ref, b_ref, right_ref, left_ref, *outs):
    ways = len(outs)
    n, seqs = right_ref.shape[0], right_ref.shape[1]
    per = a_ref.shape[0] // n
    size = per + 2 * seqs
    for r in range(n):
        out, base = outs[r % ways], (r // ways) * size
        rows = slice(r * per, (r + 1) * per)
        both = a_ref[rows, :].astype(F32) + b_ref[rows, :].astype(F32)
        out[base : base + per, :] = both.astype(BF16)
        out[base + per : base + per + seqs, :] = right_ref[r]
        out[base + per + seqs : base + size, :] = left_ref[r]


def mid_body(me, *refs):
    parts, keep, send = refs[:-2], refs[-2], refs[-1]
    size = keep.shape[0]
    keep[...] = total([p[:size, :] for p in parts])
    send[...] = total([p[size:, :] for p in parts]).astype(BF16)


def row_order(me, block, n, seqs):
    rho = lax.broadcasted_iota(jnp.int32, (block, block), 0)
    col = lax.broadcasted_iota(jnp.int32, (block, block), 1)
    per = block // n
    own = per // seqs
    inner = lax.rem(rho, per)
    want = (lax.rem(inner, seqs) * n + (me[0] ^ (rho // per))) * own + inner // seqs
    return jnp.where(want == col, 1.0, 0.0).astype(BF16)


def put_rows(me, acc, n, seqs, put):
    block = acc.shape[0]
    sums = jnp.dot(
        row_order(me, block, n, seqs), acc[...].astype(BF16), preferred_element_type=F32
    ).astype(BF16)
    per = block // n
    for r in range(n):
        for t in range(per // seqs):
            for m in range(block // 128):
                slot = t * (block // 128) + m
                low = r * per + t * seqs
                put(r, slot * 128, sums[low : low + seqs, m * 128 : (m + 1) * 128])


def gate_pick(t, gs, gsc):
    for q in range(len(gs)):

        @pl.when(t == q)
        def _(q=q):
            gsc[...] = gs[q][...]


def grad_mixed_of(og_ref, gsc, block):
    return lanes(
        [
            (og_ref[u].astype(F32) * gsc[u * block : (u + 1) * block, :].astype(F32)).astype(BF16)
            for u in range(2)
        ]
    )


def cot_body(me, *refs, n):
    gs, og_ref, lt_ref, gv_ref, gm_ref, gsc = refs[:n], *refs[n:]
    block = lt_ref.shape[0]
    gate_pick(pl.program_id(0), gs, gsc)
    gm = grad_mixed_of(og_ref, gsc, block)
    gm_ref[...] = gm
    gv = jnp.dot(lt_ref[...], gm, preferred_element_type=F32).astype(BF16)
    for u in range(2):
        gv_ref[:, u] = gv[:, u * 128 : (u + 1) * 128].reshape(gv_ref.shape[0], gv_ref.shape[2], 128)


def accumulate(acc, t, add):
    @pl.when(t == 0)
    def _():
        acc[...] = add

    @pl.when(t > 0)
    def _():
        acc[...] += add


def left_body(me, gm_ref, p_ref, tie, out, acc, *, n, seqs):
    t = pl.program_id(0)
    block = acc.shape[0]
    pairs = gm_ref.shape[0]
    gm = lanes([gm_ref[v] for v in range(pairs)])
    piece = lanes([p_ref[:, u].reshape(block, 128) for u in range(2 * pairs)])
    accumulate(acc, t, lax.dot_general(gm, piece, NT, preferred_element_type=F32))

    @pl.when(t == pl.num_programs(0) - 1)
    def _():
        def put(r, low, value):
            out[r, :, low : low + 128] = value

        put_rows(me, acc, n, seqs, put)


def kernel_grad_body(me, d_ref, u_ref, k_ref, x_ref, kg_ref, gu_ref, out, scr, acc, *, heads, n, seqs):
    t = pl.program_id(0)
    step, block = u_ref.shape[0], u_ref.shape[1]

    @pl.when(t == 0)
    def _():
        def get(s, carry):
            rows = d_ref[s].astype(F32).reshape(heads * heads, 128)
            scr[pl.ds(pl.multiple_of(s * heads * heads, 256), heads * heads), :] = rows
            return carry

        lax.fori_loop(0, d_ref.shape[0], get, 0)

    gus = []
    for u in range(step):
        gv = scr[pl.ds(t * step + u, block, stride=heads), :]
        kg_ref[u] = (gv * u_ref[u].astype(F32)).astype(BF16)
        gu = (gv * k_ref[u].astype(F32)).astype(BF16)
        gu_ref[u] = gu
        gus.append(gu)
    accumulate(
        acc,
        t,
        lax.dot_general(
            lanes(gus), lanes([x_ref[u] for u in range(step)]), NT, preferred_element_type=F32
        ),
    )

    @pl.when(t == pl.num_programs(0) - 1)
    def _():
        def put(r, low, value):
            out[r, :, low : low + 128] = value

        put_rows(me, acc, n, seqs, put)


def input_grad_body(me, h_ref, gu_ref, rt_ref, out):
    block = rt_ref.shape[0]
    rhs = lanes([gu_ref[u] for u in range(2)])
    back = jnp.dot(rt_ref[...], rhs, preferred_element_type=F32)
    for u in range(2):
        rows = slice(u * block, (u + 1) * block)
        out[rows, :] = (back[:, u * 128 : (u + 1) * 128] + h_ref[rows, :].astype(F32)).astype(BF16)


def total(parts):
    return functools.reduce(lambda a, b: a + b, [p.astype(F32) for p in parts])


def pack_body(me, keep, got, out, scr, *, seqs, per):
    slots = out.shape[1]
    sums = keep[...] + got[...].astype(F32)
    weight, right, left = sums[:per], sums[per : per + seqs], sums[per + seqs :]
    blocks = sums.shape[1] // 128
    for slot in range(blocks):
        cols = slice(slot * 128, (slot + 1) * 128)
        scr[pl.ds(slot, seqs, stride=slots), :] = left[:, cols]
        scr[pl.ds(blocks + slot, seqs, stride=slots), :] = right[:, cols]
    high = seqs // 2
    zero = jnp.zeros((high, 128), F32)
    for t in range(per // high):
        for m in range(blocks):
            slot = 2 * blocks + t * blocks + m
            value = weight[t * high : (t + 1) * high, m * 128 : (m + 1) * 128]
            scr[pl.ds(slot + me[1] * slots, high, stride=2 * slots), :] = value
            scr[pl.ds(slot + (1 - me[1]) * slots, high, stride=2 * slots), :] = zero

    def emit(s, carry):
        out[s] = scr[pl.ds(pl.multiple_of(s * slots, 16), slots), :].astype(BF16)
        return carry

    lax.fori_loop(0, seqs, emit, 0)


def share_body(me, p_ref, left_ref, right_ref, weight_ref, *, factor, token):
    sums = lax.fori_loop(
        1, p_ref.shape[0], lambda s, acc: acc + p_ref[s].astype(F32), p_ref[0].astype(F32)
    )
    count = left_ref.shape[0]
    left_ref[...] = sums[:count] * factor
    right_ref[...] = sums[count : 2 * count] * factor
    weight_ref[...] = sums[2 * count :] * token


def local(inputs, out_grad, kernel, gate_weight, right_factor, left_factor):
    block = right_factor.shape[0]
    rows, width = inputs.shape
    model_width = gate_weight.shape[0]
    heads = rows // block
    seqs = block // heads
    n = model_width // width
    part = rows // n
    chan = lax.axis_index("chan")
    core = lax.axis_index("seq") % 2
    pre = jnp.stack([chan, core]).astype(jnp.int32)
    S = jax.ShapeDtypeStruct

    def swap(r, x):
        return x if r == 0 else lax.ppermute(x, "chan", [(i, i ^ r) for i in range(n)])

    def swaps(parts):
        return [swap(r, parts[r]) for r in range(n)]

    def across(x):
        return lax.ppermute(x, "seq", [(i, i ^ 1) for i in range(seqs)])

    def whole(*shape):
        return pl.BlockSpec(shape, lambda t, me: (0,) * len(shape))

    tie = pl.BlockSpec(memory_space=pl.ANY)
    mm = 2 * rows * block * width
    gg = 2 * part * model_width * model_width
    cube = rows * width * 2

    xs = lax.all_to_all(
        inputs.reshape(n, part, width), "chan", split_axis=0, concat_axis=0, tiled=True
    )
    half = lax.dynamic_slice_in_dim(gate_weight, core * (model_width // 2), model_width // 2, 0)
    near = jnp.stack([swap(r, half) for r in range(1, n)])
    far = across(near)

    x_cube = inputs.reshape(heads, block, width)
    og_cube = out_grad.reshape(heads, block, width)
    step = 4
    four = pl.BlockSpec((step, block, width), lambda g, me: (g, 0, 0))
    first, scaled = call(
        functools.partial(first_body, step=step), (heads // step,),
        [four, four, whole(block, block), tie],
        [four, whole(seqs, heads, heads, width)],
        [S((heads, block, width), BF16), S((seqs, heads, heads, width), BF16)],
        [pltpu.VMEM((block * heads, width), F32)],
        mm, 4 * cube,
    )(pre, x_cube, kernel, right_factor, far)
    piece = lax.all_to_all(scaled, "seq", split_axis=0, concat_axis=0, tiled=True)

    chunk = part // 4
    tok = pl.BlockSpec((chunk, width), lambda t, me: (t, 0))
    gate_out = call(
        functools.partial(gate_body, n=n), (part // chunk,),
        [
            pl.BlockSpec((n, chunk, width), lambda t, me: (0, t, 0)),
            whole(model_width, width),
            whole(n - 1, model_width // 2, width),
            whole(n - 1, model_width // 2, width),
        ],
        [tok] * n + [whole(model_width, model_width)],
        [S((part, width), BF16)] * n + [S((model_width, model_width), BF16)],
        [pltpu.VMEM((model_width, model_width), BF16)],
        gg, 4 * cube,
    )(pre, xs, gate_weight, near, far)
    gates_tok, wcat = gate_out[:n], gate_out[n]
    gates = swaps(gates_tok)

    pair_in = pl.BlockSpec((seqs, 2, heads, width), lambda t, me: (0, me[0] ^ t, 0, 0))
    pair_cube = pl.BlockSpec((2, block, width), lambda t, me: (me[0] ^ t, 0, 0))
    grad_mid, grad_mixed = call(
        functools.partial(cot_body, n=n), (n,),
        [whole(part, width)] * n + [pair_cube, whole(block, block)],
        [pair_in, pl.BlockSpec((None, block, 2 * width), lambda t, me: (me[0] ^ t, 0, 0))],
        [S((seqs, heads, heads, width), BF16), S((n, block, 2 * width), BF16)],
        [pltpu.VMEM((part, width), BF16)],
        mm, 4 * cube,
    )(pre, *gates, og_cube, left_factor.T)
    grad_back = lax.all_to_all(grad_mid, "seq", split_axis=0, concat_axis=0, tiled=True)

    om = call(
        mix_body, (n,),
        [pair_in, pair_cube, whole(block, block)],
        [whole(part, width)] * n,
        [S((part, width), BF16)] * n,
        [],
        mm, 3 * cube,
    )(pre, piece, og_cube, left_factor)
    oms = swaps(om)

    count = block * block // (n * seqs * 128)
    lefts = call(
        functools.partial(left_body, n=n, seqs=seqs), (n // 2,),
        [
            pl.BlockSpec((2, block, 2 * width), lambda t, me: (t, 0, 0)),
            pl.BlockSpec((seqs, 4, heads, width), lambda t, me: (0, t, 0, 0)),
            tie,
        ],
        whole(n, seqs, count * 128),
        S((n, seqs, count * 128), BF16),
        [pltpu.VMEM((block, block), F32)],
        mm, 2 * cube,
    )(pre, grad_mixed, piece, om[0])

    turned = call(
        functools.partial(turn_body, n=n, seqs=seqs), (4,),
        [whole(n, part, width)],
        pl.BlockSpec((model_width // 4, part), lambda t, me: (t, 0)),
        S((model_width, part), BF16),
        [],
        gg, 2 * cube,
    )(pre, xs)

    back_gate, grad_pre = call(
        functools.partial(back_gate_body, n=n), (part // chunk,),
        [tok] * n + [tok] * n + [whole(model_width, model_width), tie],
        [
            pl.BlockSpec((n, chunk, width), lambda t, me: (0, t, 0)),
            pl.BlockSpec((chunk, model_width), lambda t, me: (t, 0)),
        ],
        [S((n, part, width), BF16), S((part, model_width), BF16)],
        [],
        gg, 5 * cube,
    )(pre, *oms, *gates_tok, wcat, lefts)
    gate_in = lax.all_to_all(back_gate, "chan", split_axis=0, concat_axis=0, tiled=True)

    quarter = (model_width // 4, model_width)
    mine, other = call(
        functools.partial(weight_body, n=n), (4,),
        [
            pl.BlockSpec((model_width // 4, part), lambda t, me: (t, 0)),
            whole(part, model_width),
        ],
        [
            pl.BlockSpec(quarter, lambda t, me: (jnp.minimum(t, 1), 0)),
            pl.BlockSpec(quarter, lambda t, me: (jnp.maximum(t - 2, 0), 0)),
        ],
        [S((model_width // 2, model_width), BF16)] * 2,
        [],
        gg, 3 * cube,
    )(pre, turned, grad_pre)
    kernel_grad, grad_first, rights = call(
        functools.partial(kernel_grad_body, heads=heads, n=n, seqs=seqs), (heads // step,),
        [whole(seqs, heads, heads, width), four, four, four],
        [four, four, whole(n, seqs, count * 128)],
        [S((heads, block, width), BF16)] * 2 + [S((n, seqs, count * 128), BF16)],
        [pltpu.VMEM((block * heads, width), F32), pltpu.VMEM((block, block), F32)],
        mm, 6 * cube,
    )(pre, grad_back, first, kernel, x_cube)

    ways = n // 2
    per = model_width // (2 * n)
    size = per + 2 * seqs
    pieces = call(
        add_body, (1,),
        [whole(model_width // 2, model_width)] * 2 + [whole(n, seqs, count * 128)] * 2,
        [whole(2 * size, model_width)] * ways,
        [S((2 * size, model_width), BF16)] * ways,
        [],
        cube, 3 * cube,
    )(pre, mine, across(other), rights, lefts)
    keep, send = call(
        mid_body, (1,),
        [whole(2 * size, model_width)] * ways,
        [whole(size, model_width)] * 2,
        [S((size, model_width), F32), S((size, model_width), BF16)],
        [],
        cube, 2 * cube,
    )(pre, *[swap(r, pieces[r]) for r in range(ways)])

    slots = 2 * count + model_width * model_width // (n * seqs * 128)
    packed = call(
        functools.partial(pack_body, seqs=seqs, per=per), (1,),
        [whole(size, model_width)] * 2,
        whole(seqs, slots, 128),
        S((seqs, slots, 128), BF16),
        [pltpu.VMEM((seqs * slots, 128), F32)],
        cube, cube,
    )(pre, keep, swap(ways, send))
    got = lax.all_to_all(packed, "seq", split_axis=0, concat_axis=0, tiled=True)

    input_grad = call(
        input_grad_body, (n,),
        [
            pl.BlockSpec((None, part, width), lambda t, me: (t, 0, 0)),
            pl.BlockSpec((2, block, width), lambda t, me: (t, 0, 0)),
            whole(block, block),
        ],
        pl.BlockSpec((part, width), lambda t, me: (t, 0)),
        S((rows, width), BF16),
        [],
        mm, 3 * cube,
    )(pre, gate_in, grad_first, right_factor.T)

    left_share, right_share, weight_share = call(
        functools.partial(
            share_body, factor=(block * model_width) ** -0.5, token=1.0 / block
        ), (1,),
        [whole(seqs, slots, 128)],
        [whole(count, 128), whole(count, 128), whole(slots - 2 * count, 128)],
        [S((count, 128), F32), S((count, 128), F32), S((slots - 2 * count, 128), F32)],
        [],
        cube, cube,
    )(pre, got)
    return (
        input_grad,
        kernel_grad,
        right_share.reshape(-1),
        left_share.reshape(-1),
        weight_share.reshape(-1, model_width),
    )


def solution(mesh):
    in_specs = (
        P("seq", "chan"),
        P("seq", "chan"),
        P("seq", None, "chan"),
        P(None, "chan"),
        P(),
        P(),
    )
    out_specs = (
        P("seq", "chan"),
        P("seq", None, "chan"),
        P(("seq", "chan")),
        P(("seq", "chan")),
        P(("seq", "chan"), None),
    )
    return jax.shard_map(
        local, mesh=mesh, in_specs=in_specs, out_specs=out_specs, check_vma=False
    )
```

```python
import functools

import jax
import jax.numpy as jnp
from jax import lax
from jax.experimental import pallas as pl
from jax.experimental.pallas import tpu as pltpu
from jax.sharding import PartitionSpec as P


F32 = jnp.float32
BF16 = jnp.bfloat16
NT = (((1,), (1,)), ((), ()))


def call(body, grid, in_specs, out_specs, out_shape, scratch, flops, nbytes):
    return pl.pallas_call(
        body,
        grid_spec=pltpu.PrefetchScalarGridSpec(
            num_scalar_prefetch=1,
            grid=grid,
            in_specs=in_specs,
            out_specs=out_specs,
            scratch_shapes=scratch,
        ),
        out_shape=out_shape,
        cost_estimate=pl.CostEstimate(flops=flops, bytes_accessed=nbytes, transcendentals=0),
        compiler_params=pltpu.CompilerParams(vmem_limit_bytes=48 * 2**20),
    )


def lanes(parts):
    return jnp.concatenate(parts, axis=1)


def first_body(me, x_ref, k_ref, r_ref, tie, u_ref, v_ref, scr, *, step):
    g = pl.program_id(0)
    heads, block = scr.shape[0] // r_ref.shape[0], r_ref.shape[0]
    rhs = lanes([x_ref[t] for t in range(step)])
    prod = jnp.dot(r_ref[...], rhs, preferred_element_type=F32).astype(BF16)
    for t in range(step):
        u = prod[:, t * 128 : (t + 1) * 128]
        u_ref[t] = u
        v = (u.astype(F32) * k_ref[t].astype(F32)).astype(BF16)
        scr[pl.ds(g * step + t, block, stride=heads), :] = v.astype(F32)

    @pl.when(g == pl.num_programs(0) - 1)
    def _():
        def put(s, carry):
            rows = scr[pl.ds(pl.multiple_of(s * heads * heads, 256), heads * heads), :]
            v_ref[s] = rows.reshape(heads, heads, 128).astype(BF16)
            return carry

        lax.fori_loop(0, v_ref.shape[0], put, 0)


def mix_body(me, p_ref, og_ref, l_ref, *outs):
    t = pl.program_id(0)
    block = l_ref.shape[0]
    rhs = lanes([p_ref[:, u].reshape(block, 128) for u in range(2)])
    mixed = jnp.dot(l_ref[...], rhs, preferred_element_type=F32).astype(BF16).astype(F32)
    both = jnp.concatenate(
        [(og_ref[u].astype(F32) * mixed[:, u * 128 : (u + 1) * 128]).astype(BF16) for u in range(2)],
        axis=0,
    )
    for q in range(len(outs)):

        @pl.when(t == q)
        def _(q=q):
            outs[q][...] = both


def gate_body(me, x_ref, near_ref, far_ref, *refs, n):
    gs, wcat, scr = refs[:n], refs[n], refs[n + 1]

    @pl.when(pl.program_id(0) == 0)
    def _():
        half = scr.shape[0] // 2
        near = pl.ds(pl.multiple_of(me[1] * half, half), half)
        far = pl.ds(pl.multiple_of((1 - me[1]) * half, half), half)
        ways = near_ref.shape[0]
        for q in range(n):
            scr[near, q * 128 : (q + 1) * 128] = near_ref[q % ways, q // ways]
            scr[far, q * 128 : (q + 1) * 128] = far_ref[q % ways, q // ways]
        wcat[...] = scr[...]

    rows_in = lanes([x_ref[r] for r in range(n)])
    pre = jnp.dot(rows_in, scr[...], preferred_element_type=F32)
    gate = jax.nn.sigmoid(pre).astype(BF16)
    for q in range(n):
        gs[q][...] = gate[:, q * 128 : (q + 1) * 128]


def turn_body(me, x_ref, out, *, n, seqs):
    g = pl.program_id(0)
    rows, width = out.shape[0], n * 128
    rho = lax.broadcasted_iota(jnp.int32, (rows, width), 0) + g * rows
    col = lax.broadcasted_iota(jnp.int32, (rows, width), 1)
    per = width // (2 * n)
    high = seqs // 2
    own = per // high
    core = me[1] ^ (rho // (width // 2))
    rest = lax.rem(rho, width // 2)
    inner = lax.rem(rest, per)
    seq = lax.rem(inner, high) * 2 + core
    want = (seq * n + (me[0] ^ (rest // per))) * own + inner // high
    pick = jnp.where(want == col, 1.0, 0.0).astype(BF16)
    rows_in = lanes([x_ref[r] for r in range(n)])
    out[...] = lax.dot_general(pick, rows_in, NT, preferred_element_type=F32).astype(BF16)


def back_gate_body(me, *refs, n):
    os, gs, wcat = refs[:n], refs[n : 2 * n], refs[2 * n]
    hs, gp_ref, hsc = refs[2 * n + 2 : 3 * n + 2], refs[3 * n + 2], refs[3 * n + 3]
    parts = []
    for q in range(n):
        g = gs[q][...].astype(F32)
        parts.append((os[q][...].astype(F32) * g * (1.0 - g)).astype(BF16))
    gp = lanes(parts)
    gp_ref[...] = gp
    hsc[...] = lax.dot_general(gp, wcat[...], NT, preferred_element_type=F32).astype(BF16)
    for r in range(n):
        hs[r][...] = hsc[:, pl.ds(pl.multiple_of((me[0] ^ r) * 128, 128), 128)]


def weight_body(me, xt_ref, gp_ref, mine, peer, *, n):
    g = pl.program_id(0)
    w = jnp.dot(xt_ref[...], gp_ref[...], preferred_element_type=F32).astype(BF16)

    def put(out):
        for q in range(n):
            cols = pl.ds(pl.multiple_of((me[0] ^ q) * 128, 128), 128)
            out[:, cols] = w[:, q * 128 : (q + 1) * 128]

    @pl.when(g < 2)
    def _():
        put(mine)

    @pl.when(g >= 2)
    def _():
        put(peer)


def add_body(me, a_ref, b_ref, left_ref, *outs):
    per = a_ref.shape[0] // len(outs)
    for r in range(len(outs)):
        rows = slice(r * per, (r + 1) * per)
        both = a_ref[rows, :].astype(F32) + b_ref[rows, :].astype(F32)
        outs[r][:per, :] = both.astype(BF16)
        outs[r][per:, :] = left_ref[r]


def row_order(me, block, n, seqs):
    rho = lax.broadcasted_iota(jnp.int32, (block, block), 0)
    col = lax.broadcasted_iota(jnp.int32, (block, block), 1)
    per = block // n
    own = per // seqs
    inner = lax.rem(rho, per)
    want = (lax.rem(inner, seqs) * n + (me[0] ^ (rho // per))) * own + inner // seqs
    return jnp.where(want == col, 1.0, 0.0).astype(BF16)


def put_rows(me, acc, n, seqs, put):
    block = acc.shape[0]
    sums = jnp.dot(
        row_order(me, block, n, seqs), acc[...].astype(BF16), preferred_element_type=F32
    ).astype(BF16)
    per = block // n
    for r in range(n):
        for t in range(per // seqs):
            for m in range(block // 128):
                slot = t * (block // 128) + m
                low = r * per + t * seqs
                put(r, slot * 128, sums[low : low + seqs, m * 128 : (m + 1) * 128])


def gate_pick(t, gs, gsc):
    for q in range(len(gs)):

        @pl.when(t == q)
        def _(q=q):
            gsc[...] = gs[q][...]


def grad_mixed_of(og_ref, gsc, block):
    return lanes(
        [
            (og_ref[u].astype(F32) * gsc[u * block : (u + 1) * block, :].astype(F32)).astype(BF16)
            for u in range(2)
        ]
    )


def cot_body(me, *refs, n):
    gs, og_ref, lt_ref, tie, gv_ref, gm_ref, gsc = refs[:n], *refs[n:]
    block = lt_ref.shape[0]
    gate_pick(pl.program_id(0), gs, gsc)
    gm = grad_mixed_of(og_ref, gsc, block)
    gm_ref[...] = gm
    gv = jnp.dot(lt_ref[...], gm, preferred_element_type=F32).astype(BF16)
    for u in range(2):
        gv_ref[:, u] = gv[:, u * 128 : (u + 1) * 128].reshape(gv_ref.shape[0], gv_ref.shape[2], 128)


def accumulate(acc, t, add):
    @pl.when(t == 0)
    def _():
        acc[...] = add

    @pl.when(t > 0)
    def _():
        acc[...] += add


def left_body(me, gm_ref, p_ref, tie, out, acc, *, n, seqs):
    t = pl.program_id(0)
    block = acc.shape[0]
    pairs = gm_ref.shape[0]
    gm = lanes([gm_ref[v] for v in range(pairs)])
    piece = lanes([p_ref[:, u].reshape(block, 128) for u in range(2 * pairs)])
    accumulate(acc, t, lax.dot_general(gm, piece, NT, preferred_element_type=F32))

    @pl.when(t == pl.num_programs(0) - 1)
    def _():
        def put(r, low, value):
            out[r, :, low : low + 128] = value

        put_rows(me, acc, n, seqs, put)


def kernel_grad_body(me, d_ref, u_ref, k_ref, x_ref, kg_ref, gu_ref, *refs, heads, n, seqs):
    outs, scr, acc = refs[:n], refs[n], refs[n + 1]
    t = pl.program_id(0)
    step, block = u_ref.shape[0], u_ref.shape[1]

    @pl.when(t == 0)
    def _():
        def get(s, carry):
            rows = d_ref[s].astype(F32).reshape(heads * heads, 128)
            scr[pl.ds(pl.multiple_of(s * heads * heads, 256), heads * heads), :] = rows
            return carry

        lax.fori_loop(0, d_ref.shape[0], get, 0)

    gus = []
    for u in range(step):
        gv = scr[pl.ds(t * step + u, block, stride=heads), :]
        kg_ref[u] = (gv * u_ref[u].astype(F32)).astype(BF16)
        gu = (gv * k_ref[u].astype(F32)).astype(BF16)
        gu_ref[u] = gu
        gus.append(gu)
    accumulate(
        acc,
        t,
        lax.dot_general(
            lanes(gus), lanes([x_ref[u] for u in range(step)]), NT, preferred_element_type=F32
        ),
    )

    @pl.when(t == pl.num_programs(0) - 1)
    def _():
        def put(r, low, value):
            outs[r][:, low : low + 128] = value

        put_rows(me, acc, n, seqs, put)


def input_grad_body(me, *refs, n):
    hs, gu_ref, rt_ref, out, hsc = refs[:n], refs[n], refs[n + 1], refs[n + 2], refs[n + 3]
    block = rt_ref.shape[0]
    gate_pick(pl.program_id(0), hs, hsc)
    rhs = lanes([gu_ref[u] for u in range(2)])
    back = jnp.dot(rt_ref[...], rhs, preferred_element_type=F32)
    for u in range(2):
        rows = slice(u * block, (u + 1) * block)
        out[rows, :] = (back[:, u * 128 : (u + 1) * 128] + hsc[rows, :].astype(F32)).astype(BF16)


def total(parts):
    return functools.reduce(lambda a, b: a + b, [p.astype(F32) for p in parts])


def pack_body(me, *refs, n, seqs, per):
    out, scr = refs[2 * n], refs[2 * n + 1]
    slots = out.shape[1]
    sums = total([p[...] for p in refs[:n]])
    right = total([p[...] for p in refs[n : 2 * n]])
    weight, left = sums[:per], sums[per:]
    blocks = sums.shape[1] // 128
    for slot in range(blocks):
        cols = slice(slot * 128, (slot + 1) * 128)
        scr[pl.ds(slot, seqs, stride=slots), :] = left[:, cols]
        scr[pl.ds(blocks + slot, seqs, stride=slots), :] = right[:, cols]
    high = seqs // 2
    zero = jnp.zeros((high, 128), F32)
    for t in range(per // high):
        for m in range(blocks):
            slot = 2 * blocks + t * blocks + m
            value = weight[t * high : (t + 1) * high, m * 128 : (m + 1) * 128]
            scr[pl.ds(slot + me[1] * slots, high, stride=2 * slots), :] = value
            scr[pl.ds(slot + (1 - me[1]) * slots, high, stride=2 * slots), :] = zero

    def emit(s, carry):
        out[s] = scr[pl.ds(pl.multiple_of(s * slots, 16), slots), :].astype(BF16)
        return carry

    lax.fori_loop(0, seqs, emit, 0)


def share_body(me, p_ref, left_ref, right_ref, weight_ref, *, factor, token):
    sums = lax.fori_loop(
        1, p_ref.shape[0], lambda s, acc: acc + p_ref[s].astype(F32), p_ref[0].astype(F32)
    )
    count = left_ref.shape[0]
    left_ref[...] = sums[:count] * factor
    right_ref[...] = sums[count : 2 * count] * factor
    weight_ref[...] = sums[2 * count :] * token


def local(inputs, out_grad, kernel, gate_weight, right_factor, left_factor):
    block = right_factor.shape[0]
    rows, width = inputs.shape
    model_width = gate_weight.shape[0]
    heads = rows // block
    seqs = block // heads
    n = model_width // width
    part = rows // n
    chan = lax.axis_index("chan")
    core = lax.axis_index("seq") % 2
    pre = jnp.stack([chan, core]).astype(jnp.int32)
    S = jax.ShapeDtypeStruct

    def swap(r, x):
        return x if r == 0 else lax.ppermute(x, "chan", [(i, i ^ r) for i in range(n)])

    def swaps(parts):
        return [swap(r, parts[r]) for r in range(n)]

    def across(x):
        return lax.ppermute(x, "seq", [(i, i ^ 1) for i in range(seqs)])

    def whole(*shape):
        return pl.BlockSpec(shape, lambda t, me: (0,) * len(shape))

    tie = pl.BlockSpec(memory_space=pl.ANY)
    mm = 2 * rows * block * width
    gg = 2 * part * model_width * model_width
    cube = rows * width * 2

    xs = lax.all_to_all(
        inputs.reshape(n, part, width), "chan", split_axis=0, concat_axis=0, tiled=True
    )
    half = lax.dynamic_slice_in_dim(gate_weight, core * (model_width // 2), model_width // 2, 0)
    ways = n // 2
    halves = jnp.stack([half, swap(ways, half)])
    near = jnp.stack([swap(r, halves) for r in range(ways)])
    far = across(near)

    x_cube = inputs.reshape(heads, block, width)
    og_cube = out_grad.reshape(heads, block, width)
    step = 4
    four = pl.BlockSpec((step, block, width), lambda g, me: (g, 0, 0))
    first, scaled = call(
        functools.partial(first_body, step=step), (heads // step,),
        [four, four, whole(block, block), tie],
        [four, whole(seqs, heads, heads, width)],
        [S((heads, block, width), BF16), S((seqs, heads, heads, width), BF16)],
        [pltpu.VMEM((block * heads, width), F32)],
        mm, 4 * cube,
    )(pre, x_cube, kernel, right_factor, far)
    piece = lax.all_to_all(scaled, "seq", split_axis=0, concat_axis=0, tiled=True)

    chunk = part // 4
    tok = pl.BlockSpec((chunk, width), lambda t, me: (t, 0))
    gate_out = call(
        functools.partial(gate_body, n=n), (part // chunk,),
        [
            pl.BlockSpec((n, chunk, width), lambda t, me: (0, t, 0)),
            whole(n // 2, 2, model_width // 2, width),
            whole(n // 2, 2, model_width // 2, width),
        ],
        [tok] * n + [whole(model_width, model_width)],
        [S((part, width), BF16)] * n + [S((model_width, model_width), BF16)],
        [pltpu.VMEM((model_width, model_width), BF16)],
        gg, 4 * cube,
    )(pre, xs, near, far)
    gates_tok, wcat = gate_out[:n], gate_out[n]
    gates = swaps(gates_tok)

    pair_in = pl.BlockSpec((seqs, 2, heads, width), lambda t, me: (0, me[0] ^ t, 0, 0))
    pair_cube = pl.BlockSpec((2, block, width), lambda t, me: (me[0] ^ t, 0, 0))
    om = call(
        mix_body, (n,),
        [pair_in, pair_cube, whole(block, block)],
        [whole(part, width)] * n,
        [S((part, width), BF16)] * n,
        [],
        mm, 3 * cube,
    )(pre, piece, og_cube, left_factor)
    oms = swaps(om)

    grad_mid, grad_mixed = call(
        functools.partial(cot_body, n=n), (n,),
        [whole(part, width)] * n + [pair_cube, whole(block, block), tie],
        [pair_in, pl.BlockSpec((None, block, 2 * width), lambda t, me: (me[0] ^ t, 0, 0))],
        [S((seqs, heads, heads, width), BF16), S((n, block, 2 * width), BF16)],
        [pltpu.VMEM((part, width), BF16)],
        mm, 4 * cube,
    )(pre, *gates, og_cube, left_factor.T, om[0])
    grad_back = lax.all_to_all(grad_mid, "seq", split_axis=0, concat_axis=0, tiled=True)

    count = block * block // (n * seqs * 128)
    lefts = call(
        functools.partial(left_body, n=n, seqs=seqs), (n // 2,),
        [
            pl.BlockSpec((2, block, 2 * width), lambda t, me: (t, 0, 0)),
            pl.BlockSpec((seqs, 4, heads, width), lambda t, me: (0, t, 0, 0)),
            tie,
        ],
        whole(n, seqs, count * 128),
        S((n, seqs, count * 128), BF16),
        [pltpu.VMEM((block, block), F32)],
        mm, 2 * cube,
    )(pre, grad_mixed, piece, om[0])

    turned = call(
        functools.partial(turn_body, n=n, seqs=seqs), (4,),
        [whole(n, part, width)],
        pl.BlockSpec((model_width // 4, part), lambda t, me: (t, 0)),
        S((model_width, part), BF16),
        [],
        gg, 2 * cube,
    )(pre, xs)

    back_out = call(
        functools.partial(back_gate_body, n=n), (part // chunk,),
        [tok] * n + [tok] * n + [whole(model_width, model_width), tie],
        [tok] * n + [pl.BlockSpec((chunk, model_width), lambda t, me: (t, 0))],
        [S((part, width), BF16)] * n + [S((part, model_width), BF16)],
        [pltpu.VMEM((chunk, model_width), BF16)],
        gg, 5 * cube,
    )(pre, *oms, *gates_tok, wcat, lefts)
    grad_pre = back_out[n]

    quarter = (model_width // 4, model_width)
    mine, other = call(
        functools.partial(weight_body, n=n), (4,),
        [
            pl.BlockSpec((model_width // 4, part), lambda t, me: (t, 0)),
            whole(part, model_width),
        ],
        [
            pl.BlockSpec(quarter, lambda t, me: (jnp.minimum(t, 1), 0)),
            pl.BlockSpec(quarter, lambda t, me: (jnp.maximum(t - 2, 0), 0)),
        ],
        [S((model_width // 2, model_width), BF16)] * 2,
        [],
        gg, 3 * cube,
    )(pre, turned, grad_pre)
    per = model_width // (2 * n)
    size = per + seqs
    sums_out = call(
        add_body, (1,),
        [whole(model_width // 2, model_width)] * 2 + [whole(n, seqs, count * 128)],
        [whole(size, model_width)] * n,
        [S((size, model_width), BF16)] * n,
        [],
        cube, 2 * cube,
    )(pre, mine, across(other), lefts)
    sums = swaps(sums_out)
    hs = swaps(back_out[:n])

    kernel_out = call(
        functools.partial(kernel_grad_body, heads=heads, n=n, seqs=seqs), (heads // step,),
        [whole(seqs, heads, heads, width), four, four, four],
        [four, four] + [whole(seqs, count * 128)] * n,
        [S((heads, block, width), BF16)] * 2 + [S((seqs, count * 128), BF16)] * n,
        [pltpu.VMEM((block * heads, width), F32), pltpu.VMEM((block, block), F32)],
        mm, 6 * cube,
    )(pre, grad_back, first, kernel, x_cube)

    kernel_grad, grad_first = kernel_out[:2]
    rights = swaps(kernel_out[2:])

    slots = 2 * count + model_width * model_width // (n * seqs * 128)
    packed = call(
        functools.partial(pack_body, n=n, seqs=seqs, per=per), (1,),
        [whole(size, model_width)] * n + [whole(seqs, model_width)] * n,
        whole(seqs, slots, 128),
        S((seqs, slots, 128), BF16),
        [pltpu.VMEM((seqs * slots, 128), F32)],
        cube, cube,
    )(pre, *sums, *rights)
    got = lax.all_to_all(packed, "seq", split_axis=0, concat_axis=0, tiled=True)

    input_grad = call(
        functools.partial(input_grad_body, n=n), (n,),
        [whole(part, width)] * n + [pair_cube, whole(block, block)],
        pl.BlockSpec((part, width), lambda t, me: (me[0] ^ t, 0)),
        S((rows, width), BF16),
        [pltpu.VMEM((part, width), BF16)],
        mm, 3 * cube,
    )(pre, *hs, grad_first, right_factor.T)

    left_share, right_share, weight_share = call(
        functools.partial(
            share_body, factor=(block * model_width) ** -0.5, token=1.0 / block
        ), (1,),
        [whole(seqs, slots, 128)],
        [whole(count, 128), whole(count, 128), whole(slots - 2 * count, 128)],
        [S((count, 128), F32), S((count, 128), F32), S((slots - 2 * count, 128), F32)],
        [],
        cube, cube,
    )(pre, got)
    return (
        input_grad,
        kernel_grad,
        right_share.reshape(-1),
        left_share.reshape(-1),
        weight_share.reshape(-1, model_width),
    )


def solution(mesh):
    in_specs = (
        P("seq", "chan"),
        P("seq", "chan"),
        P("seq", None, "chan"),
        P(None, "chan"),
        P(),
        P(),
    )
    out_specs = (
        P("seq", "chan"),
        P("seq", None, "chan"),
        P(("seq", "chan")),
        P(("seq", "chan")),
        P(("seq", "chan"), None),
    )
    return jax.shard_map(
        local, mesh=mesh, in_specs=in_specs, out_specs=out_specs, check_vma=False
    )
```

```python
import functools

import jax
import jax.numpy as jnp
from jax import lax
from jax.experimental import pallas as pl
from jax.experimental.pallas import tpu as pltpu
from jax.sharding import PartitionSpec as P


F32 = jnp.float32
BF16 = jnp.bfloat16
NT = (((1,), (1,)), ((), ()))


def call(body, grid, in_specs, out_specs, out_shape, scratch, flops, nbytes):
    return pl.pallas_call(
        body,
        grid_spec=pltpu.PrefetchScalarGridSpec(
            num_scalar_prefetch=1,
            grid=grid,
            in_specs=in_specs,
            out_specs=out_specs,
            scratch_shapes=scratch,
        ),
        out_shape=out_shape,
        cost_estimate=pl.CostEstimate(flops=flops, bytes_accessed=nbytes, transcendentals=0),
        compiler_params=pltpu.CompilerParams(vmem_limit_bytes=48 * 2**20),
    )


def lanes(parts):
    return jnp.concatenate(parts, axis=1)


def first_body(me, x_ref, k_ref, r_ref, u_ref, v_ref, scr, *, step):
    g = pl.program_id(0)
    heads, block = scr.shape[0] // r_ref.shape[0], r_ref.shape[0]
    rhs = lanes([x_ref[t] for t in range(step)])
    prod = jnp.dot(r_ref[...], rhs, preferred_element_type=F32).astype(BF16)
    for t in range(step):
        u = prod[:, t * 128 : (t + 1) * 128]
        u_ref[t] = u
        v = (u.astype(F32) * k_ref[t].astype(F32)).astype(BF16)
        scr[pl.ds(g * step + t, block, stride=heads), :] = v.astype(F32)

    @pl.when(g == pl.num_programs(0) - 1)
    def _():
        def put(s, carry):
            rows = scr[pl.ds(pl.multiple_of(s * heads * heads, 256), heads * heads), :]
            v_ref[s] = rows.reshape(heads, heads, 128).astype(BF16)
            return carry

        lax.fori_loop(0, v_ref.shape[0], put, 0)


def mix_body(me, p_ref, og_ref, l_ref, *outs):
    t = pl.program_id(0)
    block = l_ref.shape[0]
    rhs = lanes([p_ref[:, u].reshape(block, 128) for u in range(2)])
    mixed = jnp.dot(l_ref[...], rhs, preferred_element_type=F32).astype(BF16).astype(F32)
    both = jnp.concatenate(
        [(og_ref[u].astype(F32) * mixed[:, u * 128 : (u + 1) * 128]).astype(BF16) for u in range(2)],
        axis=0,
    )
    for q in range(len(outs)):

        @pl.when(t == q)
        def _(q=q):
            outs[q][...] = both


def gate_body(me, x_ref, *refs, n):
    quads, gs, wcat, scr = refs[:4], refs[4 : 4 + n], refs[4 + n], refs[5 + n]

    @pl.when(pl.program_id(0) == 0)
    def _():
        quarter = scr.shape[0] // 4
        ways = quads[0].shape[0]
        for k in range(4):
            spot = (me[1] ^ (k // 2)) * 2 + (me[2] ^ (k % 2))
            rows = pl.ds(pl.multiple_of(spot * quarter, quarter), quarter)
            for q in range(n):
                scr[rows, q * 128 : (q + 1) * 128] = quads[k][q % ways, q // ways]
        wcat[...] = scr[...]

    rows_in = lanes([x_ref[r] for r in range(n)])
    pre = jnp.dot(rows_in, scr[...], preferred_element_type=F32)
    gate = jax.nn.sigmoid(pre).astype(BF16)
    for q in range(n):
        gs[q][...] = gate[:, q * 128 : (q + 1) * 128]


def turn_body(me, x_ref, out, *, n, seqs):
    g = pl.program_id(0)
    rows, width = out.shape[0], n * 128
    rho = lax.broadcasted_iota(jnp.int32, (rows, width), 0) + g * rows
    col = lax.broadcasted_iota(jnp.int32, (rows, width), 1)
    per = width // (2 * n)
    high = seqs // 2
    own = per // high
    core = me[1] ^ (rho // (width // 2))
    rest = lax.rem(rho, width // 2)
    inner = lax.rem(rest, per)
    seq = lax.rem(inner, high) * 2 + core
    want = (seq * n + (me[0] ^ (rest // per))) * own + inner // high
    pick = jnp.where(want == col, 1.0, 0.0).astype(BF16)
    rows_in = lanes([x_ref[r] for r in range(n)])
    out[...] = lax.dot_general(pick, rows_in, NT, preferred_element_type=F32).astype(BF16)


def back_gate_body(me, *refs, n):
    os, gs, wcat = refs[:n], refs[n : 2 * n], refs[2 * n]
    hs, gp_ref, hsc = refs[2 * n + 2 : 3 * n + 2], refs[3 * n + 2], refs[3 * n + 3]
    parts = []
    for q in range(n):
        g = gs[q][...].astype(F32)
        parts.append((os[q][...].astype(F32) * g * (1.0 - g)).astype(BF16))
    gp = lanes(parts)
    gp_ref[...] = gp
    hsc[...] = lax.dot_general(gp, wcat[...], NT, preferred_element_type=F32).astype(BF16)
    for r in range(n):
        hs[r][...] = hsc[:, pl.ds(pl.multiple_of((me[0] ^ r) * 128, 128), 128)]


def weight_body(me, xt_ref, gp_ref, mine, peer, *, n):
    g = pl.program_id(0)
    w = jnp.dot(xt_ref[...], gp_ref[...], preferred_element_type=F32).astype(BF16)

    def put(out):
        for q in range(n):
            cols = pl.ds(pl.multiple_of((me[0] ^ q) * 128, 128), 128)
            out[:, cols] = w[:, q * 128 : (q + 1) * 128]

    @pl.when(g < 2)
    def _():
        put(mine)

    @pl.when(g >= 2)
    def _():
        put(peer)


def add_body(me, a_ref, b_ref, left_ref, *outs):
    n, seqs = left_ref.shape[0], left_ref.shape[1]
    per = a_ref.shape[0] // n
    for r in range(n):
        out, base = outs[r % len(outs)], (r // len(outs)) * (per + seqs)
        rows = slice(r * per, (r + 1) * per)
        both = a_ref[rows, :].astype(F32) + b_ref[rows, :].astype(F32)
        out[base : base + per, :] = both.astype(BF16)
        out[base + per : base + per + seqs, :] = left_ref[r]


def mid_body(me, *refs, ways):
    keep, send = refs[2 * ways :]
    low = 0
    for group in (refs[:ways], refs[ways : 2 * ways]):
        size = group[0].shape[0] // 2
        keep[low : low + size, :] = total([p[:size, :] for p in group])
        send[low : low + size, :] = total([p[size:, :] for p in group]).astype(BF16)
        low += size


def row_order(me, block, n, seqs):
    rho = lax.broadcasted_iota(jnp.int32, (block, block), 0)
    col = lax.broadcasted_iota(jnp.int32, (block, block), 1)
    per = block // n
    own = per // seqs
    inner = lax.rem(rho, per)
    want = (lax.rem(inner, seqs) * n + (me[0] ^ (rho // per))) * own + inner // seqs
    return jnp.where(want == col, 1.0, 0.0).astype(BF16)


def put_rows(me, acc, n, seqs, put):
    block = acc.shape[0]
    sums = jnp.dot(
        row_order(me, block, n, seqs), acc[...].astype(BF16), preferred_element_type=F32
    ).astype(BF16)
    per = block // n
    for r in range(n):
        for t in range(per // seqs):
            for m in range(block // 128):
                slot = t * (block // 128) + m
                low = r * per + t * seqs
                put(r, slot * 128, sums[low : low + seqs, m * 128 : (m + 1) * 128])


def gate_pick(t, gs, gsc):
    for q in range(len(gs)):

        @pl.when(t == q)
        def _(q=q):
            gsc[...] = gs[q][...]


def grad_mixed_of(og_ref, gsc, block):
    return lanes(
        [
            (og_ref[u].astype(F32) * gsc[u * block : (u + 1) * block, :].astype(F32)).astype(BF16)
            for u in range(2)
        ]
    )


def cot_body(me, *refs, n):
    gs, og_ref, lt_ref, tie, gv_ref, gm_ref, gsc = refs[:n], *refs[n:]
    block = lt_ref.shape[0]
    gate_pick(pl.program_id(0), gs, gsc)
    gm = grad_mixed_of(og_ref, gsc, block)
    gm_ref[...] = gm
    gv = jnp.dot(lt_ref[...], gm, preferred_element_type=F32).astype(BF16)
    for u in range(2):
        gv_ref[:, u] = gv[:, u * 128 : (u + 1) * 128].reshape(gv_ref.shape[0], gv_ref.shape[2], 128)


def accumulate(acc, t, add):
    @pl.when(t == 0)
    def _():
        acc[...] = add

    @pl.when(t > 0)
    def _():
        acc[...] += add


def left_body(me, gm_ref, p_ref, tie, out, acc, *, n, seqs):
    t = pl.program_id(0)
    block = acc.shape[0]
    pairs = gm_ref.shape[0]
    gm = lanes([gm_ref[v] for v in range(pairs)])
    piece = lanes([p_ref[:, u].reshape(block, 128) for u in range(2 * pairs)])
    accumulate(acc, t, lax.dot_general(gm, piece, NT, preferred_element_type=F32))

    @pl.when(t == pl.num_programs(0) - 1)
    def _():
        def put(r, low, value):
            out[r, :, low : low + 128] = value

        put_rows(me, acc, n, seqs, put)


def kernel_grad_body(me, d_ref, u_ref, k_ref, x_ref, kg_ref, gu_ref, *refs, heads, n, seqs):
    outs, scr, acc = refs[:-2], refs[-2], refs[-1]
    t = pl.program_id(0)
    step, block = u_ref.shape[0], u_ref.shape[1]

    @pl.when(t == 0)
    def _():
        def get(s, carry):
            rows = d_ref[s].astype(F32).reshape(heads * heads, 128)
            scr[pl.ds(pl.multiple_of(s * heads * heads, 256), heads * heads), :] = rows
            return carry

        lax.fori_loop(0, d_ref.shape[0], get, 0)

    gus = []
    for u in range(step):
        gv = scr[pl.ds(t * step + u, block, stride=heads), :]
        kg_ref[u] = (gv * u_ref[u].astype(F32)).astype(BF16)
        gu = (gv * k_ref[u].astype(F32)).astype(BF16)
        gu_ref[u] = gu
        gus.append(gu)
    accumulate(
        acc,
        t,
        lax.dot_general(
            lanes(gus), lanes([x_ref[u] for u in range(step)]), NT, preferred_element_type=F32
        ),
    )

    @pl.when(t == pl.num_programs(0) - 1)
    def _():
        def put(r, low, value):
            base = (r // len(outs)) * seqs
            outs[r % len(outs)][base : base + seqs, low : low + 128] = value

        put_rows(me, acc, n, seqs, put)


def input_grad_body(me, *refs, n):
    hs, gu_ref, rt_ref, out, hsc = refs[:n], refs[n], refs[n + 1], refs[n + 2], refs[n + 3]
    block = rt_ref.shape[0]
    gate_pick(pl.program_id(0), hs, hsc)
    rhs = lanes([gu_ref[u] for u in range(2)])
    back = jnp.dot(rt_ref[...], rhs, preferred_element_type=F32)
    for u in range(2):
        rows = slice(u * block, (u + 1) * block)
        out[rows, :] = (back[:, u * 128 : (u + 1) * 128] + hsc[rows, :].astype(F32)).astype(BF16)


def total(parts):
    return functools.reduce(lambda a, b: a + b, [p.astype(F32) for p in parts])


def pack_body(me, keep, got, out, scr, *, seqs, per):
    slots = out.shape[1]
    sums = keep[...] + got[...].astype(F32)
    weight, left, right = sums[:per], sums[per : per + seqs], sums[per + seqs :]
    blocks = sums.shape[1] // 128
    for slot in range(blocks):
        cols = slice(slot * 128, (slot + 1) * 128)
        scr[pl.ds(slot, seqs, stride=slots), :] = left[:, cols]
        scr[pl.ds(blocks + slot, seqs, stride=slots), :] = right[:, cols]
    high = seqs // 2
    zero = jnp.zeros((high, 128), F32)
    for t in range(per // high):
        for m in range(blocks):
            slot = 2 * blocks + t * blocks + m
            value = weight[t * high : (t + 1) * high, m * 128 : (m + 1) * 128]
            scr[pl.ds(slot + me[1] * slots, high, stride=2 * slots), :] = value
            scr[pl.ds(slot + (1 - me[1]) * slots, high, stride=2 * slots), :] = zero

    def emit(s, carry):
        out[s] = scr[pl.ds(pl.multiple_of(s * slots, 16), slots), :].astype(BF16)
        return carry

    lax.fori_loop(0, seqs, emit, 0)


def share_body(me, p_ref, left_ref, right_ref, weight_ref, *, factor, token):
    sums = lax.fori_loop(
        1, p_ref.shape[0], lambda s, acc: acc + p_ref[s].astype(F32), p_ref[0].astype(F32)
    )
    count = left_ref.shape[0]
    left_ref[...] = sums[:count] * factor
    right_ref[...] = sums[count : 2 * count] * factor
    weight_ref[...] = sums[2 * count :] * token


def local(inputs, out_grad, kernel, gate_weight, right_factor, left_factor):
    block = right_factor.shape[0]
    rows, width = inputs.shape
    model_width = gate_weight.shape[0]
    heads = rows // block
    seqs = block // heads
    n = model_width // width
    part = rows // n
    chan = lax.axis_index("chan")
    seq = lax.axis_index("seq")
    core, side = seq % 2, (seq // 2) % 2
    pre = jnp.stack([chan, core, side]).astype(jnp.int32)
    S = jax.ShapeDtypeStruct

    def swap(r, x):
        return x if r == 0 else lax.ppermute(x, "chan", [(i, i ^ r) for i in range(n)])

    def swaps(parts):
        return [swap(r, parts[r]) for r in range(n)]

    def across(x, bit=1):
        return lax.ppermute(x, "seq", [(i, i ^ bit) for i in range(seqs)])

    def whole(*shape):
        return pl.BlockSpec(shape, lambda t, me: (0,) * len(shape))

    tie = pl.BlockSpec(memory_space=pl.ANY)
    mm = 2 * rows * block * width
    gg = 2 * part * model_width * model_width
    cube = rows * width * 2

    xs = lax.all_to_all(
        inputs.reshape(n, part, width), "chan", split_axis=0, concat_axis=0, tiled=True
    )
    quarter = model_width // 4
    slab = lax.dynamic_slice_in_dim(gate_weight, (core * 2 + side) * quarter, quarter, 0)
    ways = n // 2
    slabs = jnp.stack([slab, swap(ways, slab)])
    near = jnp.stack([swap(r, slabs) for r in range(ways)])
    beside = across(near, 2)
    quads = [near, beside, across(near), across(beside)]

    x_cube = inputs.reshape(heads, block, width)
    og_cube = out_grad.reshape(heads, block, width)
    step = 4
    four = pl.BlockSpec((step, block, width), lambda g, me: (g, 0, 0))
    first, scaled = call(
        functools.partial(first_body, step=step), (heads // step,),
        [four, four, whole(block, block)],
        [four, whole(seqs, heads, heads, width)],
        [S((heads, block, width), BF16), S((seqs, heads, heads, width), BF16)],
        [pltpu.VMEM((block * heads, width), F32)],
        mm, 4 * cube,
    )(pre, x_cube, kernel, right_factor)
    piece = lax.all_to_all(scaled, "seq", split_axis=0, concat_axis=0, tiled=True)

    chunk = part // 4
    tok = pl.BlockSpec((chunk, width), lambda t, me: (t, 0))
    gate_out = call(
        functools.partial(gate_body, n=n), (part // chunk,),
        [
            pl.BlockSpec((n, chunk, width), lambda t, me: (0, t, 0)),
        ]
        + [whole(n // 2, 2, model_width // 4, width)] * 4,
        [tok] * n + [whole(model_width, model_width)],
        [S((part, width), BF16)] * n + [S((model_width, model_width), BF16)],
        [pltpu.VMEM((model_width, model_width), BF16)],
        gg, 4 * cube,
    )(pre, xs, *quads)
    gates_tok, wcat = gate_out[:n], gate_out[n]
    gates = swaps(gates_tok)

    pair_in = pl.BlockSpec((seqs, 2, heads, width), lambda t, me: (0, me[0] ^ t, 0, 0))
    pair_cube = pl.BlockSpec((2, block, width), lambda t, me: (me[0] ^ t, 0, 0))
    om = call(
        mix_body, (n,),
        [pair_in, pair_cube, whole(block, block)],
        [whole(part, width)] * n,
        [S((part, width), BF16)] * n,
        [],
        mm, 3 * cube,
    )(pre, piece, og_cube, left_factor)
    oms = swaps(om)

    grad_mid, grad_mixed = call(
        functools.partial(cot_body, n=n), (n,),
        [whole(part, width)] * n + [pair_cube, whole(block, block), tie],
        [pair_in, pl.BlockSpec((None, block, 2 * width), lambda t, me: (me[0] ^ t, 0, 0))],
        [S((seqs, heads, heads, width), BF16), S((n, block, 2 * width), BF16)],
        [pltpu.VMEM((part, width), BF16)],
        mm, 4 * cube,
    )(pre, *gates, og_cube, left_factor.T, om[0])
    grad_back = lax.all_to_all(grad_mid, "seq", split_axis=0, concat_axis=0, tiled=True)

    count = block * block // (n * seqs * 128)
    lefts = call(
        functools.partial(left_body, n=n, seqs=seqs), (n // 2,),
        [
            pl.BlockSpec((2, block, 2 * width), lambda t, me: (t, 0, 0)),
            pl.BlockSpec((seqs, 4, heads, width), lambda t, me: (0, t, 0, 0)),
            tie,
        ],
        whole(n, seqs, count * 128),
        S((n, seqs, count * 128), BF16),
        [pltpu.VMEM((block, block), F32)],
        mm, 2 * cube,
    )(pre, grad_mixed, piece, om[0])

    turned = call(
        functools.partial(turn_body, n=n, seqs=seqs), (4,),
        [whole(n, part, width)],
        pl.BlockSpec((model_width // 4, part), lambda t, me: (t, 0)),
        S((model_width, part), BF16),
        [],
        gg, 2 * cube,
    )(pre, xs)

    back_out = call(
        functools.partial(back_gate_body, n=n), (part // chunk,),
        [tok] * n + [tok] * n + [whole(model_width, model_width), tie],
        [tok] * n + [pl.BlockSpec((chunk, model_width), lambda t, me: (t, 0))],
        [S((part, width), BF16)] * n + [S((part, model_width), BF16)],
        [pltpu.VMEM((chunk, model_width), BF16)],
        gg, 5 * cube,
    )(pre, *oms, *gates_tok, wcat, lefts)
    grad_pre = back_out[n]

    strip = (model_width // 4, model_width)
    mine, other = call(
        functools.partial(weight_body, n=n), (4,),
        [
            pl.BlockSpec((model_width // 4, part), lambda t, me: (t, 0)),
            whole(part, model_width),
        ],
        [
            pl.BlockSpec(strip, lambda t, me: (jnp.minimum(t, 1), 0)),
            pl.BlockSpec(strip, lambda t, me: (jnp.maximum(t - 2, 0), 0)),
        ],
        [S((model_width // 2, model_width), BF16)] * 2,
        [],
        gg, 3 * cube,
    )(pre, turned, grad_pre)
    per = model_width // (2 * n)
    size = per + seqs
    sums_out = call(
        add_body, (1,),
        [whole(model_width // 2, model_width)] * 2 + [whole(n, seqs, count * 128)],
        [whole(2 * size, model_width)] * ways,
        [S((2 * size, model_width), BF16)] * ways,
        [],
        cube, 2 * cube,
    )(pre, mine, across(other), lefts)
    sums = [swap(r, sums_out[r]) for r in range(ways)]
    hs = swaps(back_out[:n])

    kernel_out = call(
        functools.partial(kernel_grad_body, heads=heads, n=n, seqs=seqs), (heads // step,),
        [whole(seqs, heads, heads, width), four, four, four],
        [four, four] + [whole(2 * seqs, count * 128)] * ways,
        [S((heads, block, width), BF16)] * 2 + [S((2 * seqs, count * 128), BF16)] * ways,
        [pltpu.VMEM((block * heads, width), F32), pltpu.VMEM((block, block), F32)],
        mm, 6 * cube,
    )(pre, grad_back, first, kernel, x_cube)

    kernel_grad, grad_first = kernel_out[:2]
    rights = [swap(r, kernel_out[2 + r]) for r in range(ways)]
    whole_size = size + seqs
    keep, send = call(
        functools.partial(mid_body, ways=ways), (1,),
        [whole(2 * size, model_width)] * ways + [whole(2 * seqs, model_width)] * ways,
        [whole(whole_size, model_width)] * 2,
        [S((whole_size, model_width), F32), S((whole_size, model_width), BF16)],
        [],
        cube, 2 * cube,
    )(pre, *sums, *rights)

    slots = 2 * count + model_width * model_width // (n * seqs * 128)
    packed = call(
        functools.partial(pack_body, seqs=seqs, per=per), (1,),
        [whole(whole_size, model_width)] * 2,
        whole(seqs, slots, 128),
        S((seqs, slots, 128), BF16),
        [pltpu.VMEM((seqs * slots, 128), F32)],
        cube, cube,
    )(pre, keep, swap(ways, send))
    got = lax.all_to_all(packed, "seq", split_axis=0, concat_axis=0, tiled=True)

    input_grad = call(
        functools.partial(input_grad_body, n=n), (n,),
        [whole(part, width)] * n + [pair_cube, whole(block, block)],
        pl.BlockSpec((part, width), lambda t, me: (me[0] ^ t, 0)),
        S((rows, width), BF16),
        [pltpu.VMEM((part, width), BF16)],
        mm, 3 * cube,
    )(pre, *hs, grad_first, right_factor.T)

    left_share, right_share, weight_share = call(
        functools.partial(
            share_body, factor=(block * model_width) ** -0.5, token=1.0 / block
        ), (1,),
        [whole(seqs, slots, 128)],
        [whole(count, 128), whole(count, 128), whole(slots - 2 * count, 128)],
        [S((count, 128), F32), S((count, 128), F32), S((slots - 2 * count, 128), F32)],
        [],
        cube, cube,
    )(pre, got)
    return (
        input_grad,
        kernel_grad,
        right_share.reshape(-1),
        left_share.reshape(-1),
        weight_share.reshape(-1, model_width),
    )


def solution(mesh):
    in_specs = (
        P("seq", "chan"),
        P("seq", "chan"),
        P("seq", None, "chan"),
        P(None, "chan"),
        P(),
        P(),
    )
    out_specs = (
        P("seq", "chan"),
        P("seq", None, "chan"),
        P(("seq", "chan")),
        P(("seq", "chan")),
        P(("seq", "chan"), None),
    )
    return jax.shard_map(
        local, mesh=mesh, in_specs=in_specs, out_specs=out_specs, check_vma=False
    )
```

```python
import functools

import jax
import jax.numpy as jnp
from jax import lax
from jax.experimental import pallas as pl
from jax.experimental.pallas import tpu as pltpu
from jax.sharding import PartitionSpec as P


F32 = jnp.float32
BF16 = jnp.bfloat16
NT = (((1,), (1,)), ((), ()))


def call(body, grid, in_specs, out_specs, out_shape, scratch, flops, nbytes):
    return pl.pallas_call(
        body,
        grid_spec=pltpu.PrefetchScalarGridSpec(
            num_scalar_prefetch=1,
            grid=grid,
            in_specs=in_specs,
            out_specs=out_specs,
            scratch_shapes=scratch,
        ),
        out_shape=out_shape,
        cost_estimate=pl.CostEstimate(flops=flops, bytes_accessed=nbytes, transcendentals=0),
        compiler_params=pltpu.CompilerParams(vmem_limit_bytes=48 * 2**20),
    )


def lanes(parts):
    return jnp.concatenate(parts, axis=1)


def first_body(me, x_ref, k_ref, r_ref, u_ref, v_ref, scr, *, step):
    g = pl.program_id(0)
    heads, block = scr.shape[0] // r_ref.shape[0], r_ref.shape[0]
    rhs = lanes([x_ref[t] for t in range(step)])
    prod = jnp.dot(r_ref[...], rhs, preferred_element_type=F32).astype(BF16)
    for t in range(step):
        u = prod[:, t * 128 : (t + 1) * 128]
        u_ref[t] = u
        v = (u.astype(F32) * k_ref[t].astype(F32)).astype(BF16)
        scr[pl.ds(g * step + t, block, stride=heads), :] = v.astype(F32)

    @pl.when(g == pl.num_programs(0) - 1)
    def _():
        def put(s, carry):
            rows = scr[pl.ds(pl.multiple_of(s * heads * heads, 256), heads * heads), :]
            v_ref[s] = rows.reshape(heads, heads, 128).astype(BF16)
            return carry

        lax.fori_loop(0, v_ref.shape[0], put, 0)


def mix_body(me, p_ref, og_ref, l_ref, *outs):
    t = pl.program_id(0)
    block = l_ref.shape[0]
    rhs = lanes([p_ref[:, u].reshape(block, 128) for u in range(2)])
    mixed = jnp.dot(l_ref[...], rhs, preferred_element_type=F32).astype(BF16).astype(F32)
    both = jnp.concatenate(
        [(og_ref[u].astype(F32) * mixed[:, u * 128 : (u + 1) * 128]).astype(BF16) for u in range(2)],
        axis=0,
    )
    for q in range(len(outs)):

        @pl.when(t == q)
        def _(q=q):
            outs[q][...] = both


def gate_body(me, x_ref, *refs, n):
    quads, gs, wcat, scr = refs[:4], refs[4 : 4 + n], refs[4 + n], refs[5 + n]

    @pl.when(pl.program_id(0) == 0)
    def _():
        quarter = scr.shape[0] // 4
        ways = quads[0].shape[0]
        for k in range(4):
            spot = (me[1] ^ (k // 2)) * 2 + (me[2] ^ (k % 2))
            rows = pl.ds(pl.multiple_of(spot * quarter, quarter), quarter)
            for q in range(n):
                scr[rows, q * 128 : (q + 1) * 128] = quads[k][q % ways, q // ways]
        wcat[...] = scr[...]

    rows_in = lanes([x_ref[r] for r in range(n)])
    pre = jnp.dot(rows_in, scr[...], preferred_element_type=F32)
    gate = jax.nn.sigmoid(pre).astype(BF16)
    for q in range(n):
        gs[q][...] = gate[:, q * 128 : (q + 1) * 128]


def turn_body(me, x_ref, out, *, n, seqs):
    g = pl.program_id(0)
    rows, width = out.shape[0], n * 128
    rho = lax.broadcasted_iota(jnp.int32, (rows, width), 0) + g * rows
    col = lax.broadcasted_iota(jnp.int32, (rows, width), 1)
    per = width // (2 * n)
    high = seqs // 2
    own = per // high
    core = me[1] ^ (rho // (width // 2))
    rest = lax.rem(rho, width // 2)
    inner = lax.rem(rest, per)
    seq = lax.rem(inner, high) * 2 + core
    want = (seq * n + (me[0] ^ (rest // per))) * own + inner // high
    pick = jnp.where(want == col, 1.0, 0.0).astype(BF16)
    rows_in = lanes([x_ref[r] for r in range(n)])
    out[...] = lax.dot_general(pick, rows_in, NT, preferred_element_type=F32).astype(BF16)


def back_gate_body(me, *refs, n):
    os, gs, wcat = refs[:n], refs[n : 2 * n], refs[2 * n]
    hs, gp_ref, hsc = refs[2 * n + 2 : 3 * n + 2], refs[3 * n + 2], refs[3 * n + 3]
    parts = []
    for q in range(n):
        g = gs[q][...].astype(F32)
        parts.append((os[q][...].astype(F32) * g * (1.0 - g)).astype(BF16))
    gp = lanes(parts)
    gp_ref[...] = gp
    hsc[...] = lax.dot_general(gp, wcat[...], NT, preferred_element_type=F32).astype(BF16)
    for r in range(n):
        hs[r][...] = hsc[:, pl.ds(pl.multiple_of((me[0] ^ r) * 128, 128), 128)]


def weight_body(me, xt_ref, gp_ref, mine, peer, *, n):
    g = pl.program_id(0)
    w = jnp.dot(xt_ref[...], gp_ref[...], preferred_element_type=F32).astype(BF16)

    def put(out):
        for q in range(n):
            cols = pl.ds(pl.multiple_of((me[0] ^ q) * 128, 128), 128)
            out[:, cols] = w[:, q * 128 : (q + 1) * 128]

    @pl.when(g < 2)
    def _():
        put(mine)

    @pl.when(g >= 2)
    def _():
        put(peer)


def add_body(me, a_ref, b_ref, left_ref, *outs):
    n, seqs = left_ref.shape[0], left_ref.shape[1]
    per = a_ref.shape[0] // n
    for r in range(n):
        out, base = outs[r % len(outs)], (r // len(outs)) * (per + seqs)
        rows = slice(r * per, (r + 1) * per)
        both = a_ref[rows, :].astype(F32) + b_ref[rows, :].astype(F32)
        out[base : base + per, :] = both.astype(BF16)
        out[base + per : base + per + seqs, :] = left_ref[r]


def mid_body(me, *refs, ways):
    keep, send = refs[2 * ways :]
    low = 0
    for group in (refs[:ways], refs[ways : 2 * ways]):
        size = group[0].shape[0] // 2
        keep[low : low + size, :] = total([p[:size, :] for p in group])
        send[low : low + size, :] = total([p[size:, :] for p in group]).astype(BF16)
        low += size


def row_order(me, block, n, seqs):
    rho = lax.broadcasted_iota(jnp.int32, (block, block), 0)
    col = lax.broadcasted_iota(jnp.int32, (block, block), 1)
    per = block // n
    own = per // seqs
    inner = lax.rem(rho, per)
    want = (lax.rem(inner, seqs) * n + (me[0] ^ (rho // per))) * own + inner // seqs
    return jnp.where(want == col, 1.0, 0.0).astype(BF16)


def put_rows(me, acc, n, seqs, put):
    block = acc.shape[0]
    sums = jnp.dot(
        row_order(me, block, n, seqs), acc[...].astype(BF16), preferred_element_type=F32
    ).astype(BF16)
    per = block // n
    for r in range(n):
        for t in range(per // seqs):
            for m in range(block // 128):
                slot = t * (block // 128) + m
                low = r * per + t * seqs
                put(r, slot * 128, sums[low : low + seqs, m * 128 : (m + 1) * 128])


def gate_pick(t, gs, gsc):
    for q in range(len(gs)):

        @pl.when(t == q)
        def _(q=q):
            gsc[...] = gs[q][...]


def grad_mixed_of(og_ref, gsc, block):
    return lanes(
        [
            (og_ref[u].astype(F32) * gsc[u * block : (u + 1) * block, :].astype(F32)).astype(BF16)
            for u in range(2)
        ]
    )


def cot_body(me, *refs, n):
    gs, og_ref, lt_ref, tie, gv_ref, gm_ref, gsc = refs[:n], *refs[n:]
    block = lt_ref.shape[0]
    gate_pick(pl.program_id(0), gs, gsc)
    gm = grad_mixed_of(og_ref, gsc, block)
    gm_ref[...] = gm
    gv = jnp.dot(lt_ref[...], gm, preferred_element_type=F32).astype(BF16)
    for u in range(2):
        gv_ref[:, u] = gv[:, u * 128 : (u + 1) * 128].reshape(gv_ref.shape[0], gv_ref.shape[2], 128)


def accumulate(acc, t, add):
    @pl.when(t == 0)
    def _():
        acc[...] = add

    @pl.when(t > 0)
    def _():
        acc[...] += add


def left_body(me, gm_ref, p_ref, tie, out, acc, *, n, seqs):
    t = pl.program_id(0)
    block = acc.shape[0]
    pairs = gm_ref.shape[0]
    gm = lanes([gm_ref[v] for v in range(pairs)])
    piece = lanes([p_ref[:, u].reshape(block, 128) for u in range(2 * pairs)])
    accumulate(acc, t, lax.dot_general(gm, piece, NT, preferred_element_type=F32))

    @pl.when(t == pl.num_programs(0) - 1)
    def _():
        def put(r, low, value):
            out[r, :, low : low + 128] = value

        put_rows(me, acc, n, seqs, put)


def kernel_grad_body(me, d_ref, u_ref, k_ref, x_ref, kg_ref, gu_ref, *refs, heads, n, seqs):
    outs, scr, acc = refs[:-2], refs[-2], refs[-1]
    t = pl.program_id(0)
    step, block = u_ref.shape[0], u_ref.shape[1]

    @pl.when(t == 0)
    def _():
        def get(s, carry):
            rows = d_ref[s].astype(F32).reshape(heads * heads, 128)
            scr[pl.ds(pl.multiple_of(s * heads * heads, 256), heads * heads), :] = rows
            return carry

        lax.fori_loop(0, d_ref.shape[0], get, 0)

    gus = []
    for u in range(step):
        gv = scr[pl.ds(t * step + u, block, stride=heads), :]
        kg_ref[u] = (gv * u_ref[u].astype(F32)).astype(BF16)
        gu = (gv * k_ref[u].astype(F32)).astype(BF16)
        gu_ref[u] = gu
        gus.append(gu)
    accumulate(
        acc,
        t,
        lax.dot_general(
            lanes(gus), lanes([x_ref[u] for u in range(step)]), NT, preferred_element_type=F32
        ),
    )

    @pl.when(t == pl.num_programs(0) - 1)
    def _():
        def put(r, low, value):
            base = (r // len(outs)) * seqs
            outs[r % len(outs)][base : base + seqs, low : low + 128] = value

        put_rows(me, acc, n, seqs, put)


def input_grad_body(me, *refs, n):
    hs, gu_ref, rt_ref, out, hsc = refs[:n], refs[n], refs[n + 1], refs[n + 2], refs[n + 3]
    block = rt_ref.shape[0]
    gate_pick(pl.program_id(0), hs, hsc)
    rhs = lanes([gu_ref[u] for u in range(2)])
    back = jnp.dot(rt_ref[...], rhs, preferred_element_type=F32)
    for u in range(2):
        rows = slice(u * block, (u + 1) * block)
        out[rows, :] = (back[:, u * 128 : (u + 1) * 128] + hsc[rows, :].astype(F32)).astype(BF16)


def total(parts):
    return functools.reduce(lambda a, b: a + b, [p.astype(F32) for p in parts])


def pack_body(me, keep, got, out, scr, *, seqs, per):
    slots = out.shape[1]
    sums = keep[...] + got[...].astype(F32)
    weight, left, right = sums[:per], sums[per : per + seqs], sums[per + seqs :]
    blocks = sums.shape[1] // 128
    for slot in range(blocks):
        cols = slice(slot * 128, (slot + 1) * 128)
        scr[pl.ds(slot, seqs, stride=slots), :] = left[:, cols]
        scr[pl.ds(blocks + slot, seqs, stride=slots), :] = right[:, cols]
    high = seqs // 2
    zero = jnp.zeros((high, 128), F32)
    for t in range(per // high):
        for m in range(blocks):
            slot = 2 * blocks + t * blocks + m
            value = weight[t * high : (t + 1) * high, m * 128 : (m + 1) * 128]
            scr[pl.ds(slot + me[1] * slots, high, stride=2 * slots), :] = value
            scr[pl.ds(slot + (1 - me[1]) * slots, high, stride=2 * slots), :] = zero

    def emit(s, carry):
        out[s] = scr[pl.ds(pl.multiple_of(s * slots, 16), slots), :].astype(BF16)
        return carry

    lax.fori_loop(0, seqs, emit, 0)


def share_body(me, p_ref, left_ref, right_ref, weight_ref, *, factor, token):
    sums = lax.fori_loop(
        1, p_ref.shape[0], lambda s, acc: acc + p_ref[s].astype(F32), p_ref[0].astype(F32)
    )
    count = left_ref.shape[0]
    left_ref[...] = sums[:count] * factor
    right_ref[...] = sums[count : 2 * count] * factor
    weight_ref[...] = sums[2 * count :] * token


def local(inputs, out_grad, kernel, gate_weight, right_factor, left_factor):
    block = right_factor.shape[0]
    rows, width = inputs.shape
    model_width = gate_weight.shape[0]
    heads = rows // block
    seqs = block // heads
    n = model_width // width
    part = rows // n
    chan = lax.axis_index("chan")
    seq = lax.axis_index("seq")
    core, side = seq % 2, (seq // 2) % 2
    pre = jnp.stack([chan, core, side]).astype(jnp.int32)
    S = jax.ShapeDtypeStruct

    def swap(r, x):
        return x if r == 0 else lax.ppermute(x, "chan", [(i, i ^ r) for i in range(n)])

    def swaps(parts):
        return [swap(r, parts[r]) for r in range(n)]

    def across(x, bit=1):
        return lax.ppermute(x, "seq", [(i, i ^ bit) for i in range(seqs)])

    def whole(*shape):
        return pl.BlockSpec(shape, lambda t, me: (0,) * len(shape))

    tie = pl.BlockSpec(memory_space=pl.ANY)
    mm = 2 * rows * block * width
    gg = 2 * part * model_width * model_width
    cube = rows * width * 2

    xs = lax.all_to_all(
        inputs.reshape(n, part, width), "chan", split_axis=0, concat_axis=0, tiled=True
    )
    quarter = model_width // 4
    slab = lax.dynamic_slice_in_dim(gate_weight, (core * 2 + side) * quarter, quarter, 0)
    ways = n // 2
    slabs = jnp.stack([slab, swap(ways, slab)])
    near = jnp.stack([swap(r, slabs) for r in range(ways)])
    beside = across(near, 2)
    quads = [near, beside, across(near), across(beside)]

    x_cube = inputs.reshape(heads, block, width)
    og_cube = out_grad.reshape(heads, block, width)
    step = 4
    four = pl.BlockSpec((step, block, width), lambda g, me: (g, 0, 0))
    first, scaled = call(
        functools.partial(first_body, step=step), (heads // step,),
        [four, four, whole(block, block)],
        [four, whole(seqs, heads, heads, width)],
        [S((heads, block, width), BF16), S((seqs, heads, heads, width), BF16)],
        [pltpu.VMEM((block * heads, width), F32)],
        mm, 4 * cube,
    )(pre, x_cube, kernel, right_factor)
    piece = lax.all_to_all(scaled, "seq", split_axis=0, concat_axis=0, tiled=True)

    chunk = part // 4
    tok = pl.BlockSpec((chunk, width), lambda t, me: (t, 0))
    gate_out = call(
        functools.partial(gate_body, n=n), (part // chunk,),
        [
            pl.BlockSpec((n, chunk, width), lambda t, me: (0, t, 0)),
        ]
        + [whole(n // 2, 2, model_width // 4, width)] * 4,
        [tok] * n + [whole(model_width, model_width)],
        [S((part, width), BF16)] * n + [S((model_width, model_width), BF16)],
        [pltpu.VMEM((model_width, model_width), BF16)],
        gg, 4 * cube,
    )(pre, xs, *quads)
    gates_tok, wcat = gate_out[:n], gate_out[n]
    gates = swaps(gates_tok)

    pair_in = pl.BlockSpec((seqs, 2, heads, width), lambda t, me: (0, me[0] ^ t, 0, 0))
    pair_cube = pl.BlockSpec((2, block, width), lambda t, me: (me[0] ^ t, 0, 0))
    om = call(
        mix_body, (n,),
        [pair_in, pair_cube, whole(block, block)],
        [whole(part, width)] * n,
        [S((part, width), BF16)] * n,
        [],
        mm, 3 * cube,
    )(pre, piece, og_cube, left_factor)
    oms = swaps(om)

    grad_mid, grad_mixed = call(
        functools.partial(cot_body, n=n), (n,),
        [whole(part, width)] * n + [pair_cube, whole(block, block), tie],
        [pair_in, pl.BlockSpec((None, block, 2 * width), lambda t, me: (me[0] ^ t, 0, 0))],
        [S((seqs, heads, heads, width), BF16), S((n, block, 2 * width), BF16)],
        [pltpu.VMEM((part, width), BF16)],
        mm, 4 * cube,
    )(pre, *gates, og_cube, left_factor.T, om[0])
    grad_back = lax.all_to_all(grad_mid, "seq", split_axis=0, concat_axis=0, tiled=True)

    count = block * block // (n * seqs * 128)
    lefts = call(
        functools.partial(left_body, n=n, seqs=seqs), (n // 2,),
        [
            pl.BlockSpec((2, block, 2 * width), lambda t, me: (t, 0, 0)),
            pl.BlockSpec((seqs, 4, heads, width), lambda t, me: (0, t, 0, 0)),
            tie,
        ],
        whole(n, seqs, count * 128),
        S((n, seqs, count * 128), BF16),
        [pltpu.VMEM((block, block), F32)],
        mm, 2 * cube,
    )(pre, grad_mixed, piece, om[0])

    turned = call(
        functools.partial(turn_body, n=n, seqs=seqs), (4,),
        [whole(n, part, width)],
        pl.BlockSpec((model_width // 4, part), lambda t, me: (t, 0)),
        S((model_width, part), BF16),
        [],
        gg, 2 * cube,
    )(pre, xs)

    back_out = call(
        functools.partial(back_gate_body, n=n), (part // chunk,),
        [tok] * n + [tok] * n + [whole(model_width, model_width), tie],
        [tok] * n + [pl.BlockSpec((chunk, model_width), lambda t, me: (t, 0))],
        [S((part, width), BF16)] * n + [S((part, model_width), BF16)],
        [pltpu.VMEM((chunk, model_width), BF16)],
        gg, 5 * cube,
    )(pre, *oms, *gates_tok, wcat, lefts)
    grad_pre = back_out[n]

    strip = (model_width // 4, model_width)
    mine, other = call(
        functools.partial(weight_body, n=n), (4,),
        [
            pl.BlockSpec((model_width // 4, part), lambda t, me: (t, 0)),
            whole(part, model_width),
        ],
        [
            pl.BlockSpec(strip, lambda t, me: (jnp.minimum(t, 1), 0)),
            pl.BlockSpec(strip, lambda t, me: (jnp.maximum(t - 2, 0), 0)),
        ],
        [S((model_width // 2, model_width), BF16)] * 2,
        [],
        gg, 3 * cube,
    )(pre, turned, grad_pre)
    per = model_width // (2 * n)
    size = per + seqs
    sums_out = call(
        add_body, (1,),
        [whole(model_width // 2, model_width)] * 2 + [whole(n, seqs, count * 128)],
        [whole(2 * size, model_width)] * ways,
        [S((2 * size, model_width), BF16)] * ways,
        [],
        cube, 2 * cube,
    )(pre, mine, across(other), lefts)
    sums = [swap(r, sums_out[r]) for r in range(ways)]
    hs = [swap(r, back_out[r]) for r in range(ways)]
    hs += [swap(r, back_out[r]) for r in range(ways, n)]

    kernel_out = call(
        functools.partial(kernel_grad_body, heads=heads, n=n, seqs=seqs), (heads // step,),
        [whole(seqs, heads, heads, width), four, four, four],
        [four, four] + [whole(2 * seqs, count * 128)] * ways,
        [S((heads, block, width), BF16)] * 2 + [S((2 * seqs, count * 128), BF16)] * ways,
        [pltpu.VMEM((block * heads, width), F32), pltpu.VMEM((block, block), F32)],
        mm, 6 * cube,
    )(pre, grad_back, first, kernel, x_cube)

    kernel_grad, grad_first = kernel_out[:2]
    rights = [swap(r, kernel_out[2 + r]) for r in range(ways)]
    whole_size = size + seqs
    keep, send = call(
        functools.partial(mid_body, ways=ways), (1,),
        [whole(2 * size, model_width)] * ways + [whole(2 * seqs, model_width)] * ways,
        [whole(whole_size, model_width)] * 2,
        [S((whole_size, model_width), F32), S((whole_size, model_width), BF16)],
        [],
        cube, 2 * cube,
    )(pre, *sums, *rights)

    cross = swap(ways, send)
    slots = 2 * count + model_width * model_width // (n * seqs * 128)
    packed = call(
        functools.partial(pack_body, seqs=seqs, per=per), (1,),
        [whole(whole_size, model_width)] * 2,
        whole(seqs, slots, 128),
        S((seqs, slots, 128), BF16),
        [pltpu.VMEM((seqs * slots, 128), F32)],
        cube, cube,
    )(pre, keep, cross)
    got = lax.all_to_all(packed, "seq", split_axis=0, concat_axis=0, tiled=True)

    input_grad = call(
        functools.partial(input_grad_body, n=n), (n,),
        [whole(part, width)] * n + [pair_cube, whole(block, block)],
        pl.BlockSpec((part, width), lambda t, me: (me[0] ^ t, 0)),
        S((rows, width), BF16),
        [pltpu.VMEM((part, width), BF16)],
        mm, 3 * cube,
    )(pre, *hs, grad_first, right_factor.T)

    left_share, right_share, weight_share = call(
        functools.partial(
            share_body, factor=(block * model_width) ** -0.5, token=1.0 / block
        ), (1,),
        [whole(seqs, slots, 128)],
        [whole(count, 128), whole(count, 128), whole(slots - 2 * count, 128)],
        [S((count, 128), F32), S((count, 128), F32), S((slots - 2 * count, 128), F32)],
        [],
        cube, cube,
    )(pre, got)
    return (
        input_grad,
        kernel_grad,
        right_share.reshape(-1),
        left_share.reshape(-1),
        weight_share.reshape(-1, model_width),
    )


def solution(mesh):
    in_specs = (
        P("seq", "chan"),
        P("seq", "chan"),
        P("seq", None, "chan"),
        P(None, "chan"),
        P(),
        P(),
    )
    out_specs = (
        P("seq", "chan"),
        P("seq", None, "chan"),
        P(("seq", "chan")),
        P(("seq", "chan")),
        P(("seq", "chan"), None),
    )
    return jax.shard_map(
        local, mesh=mesh, in_specs=in_specs, out_specs=out_specs, check_vma=False
    )
```
